128 devices in a mesh: inline: 8 (over y, core), xline: 16 (over x, z).
Axes of the slice: x: 4, y: 4, z: 4, core: 2. Of those that a mesh axis runs over, the one named last changes fastest.
Arguments:
- traces: bfloat16 [32768, 1024], P(('inline', 'xline')), may hold values from -6 to 6
- owner: int32 [32768, 1], P(('inline', 'xline')), may hold values from 0 to 127; in each aligned block of 256 rows (0 to 255, 256 to 511, ...) at most 8 rows name the same one
- bin_ids: int32 [32768], P(('inline', 'xline')), may hold values from 0 to 323
- fold: int32 [128, 256], P('inline', 'xline'), may hold values from 1 to 8
- w_first: bfloat16 [32, 3], replicated, may hold values from -3.5 to 3.5
- w_second: bfloat16 [3, 32, 32], replicated, may hold values from -0.625 to 0.625
- w_noise: bfloat16 [32], replicated, may hold values from -1 to 1
- w_volume: bfloat16 [16, 27], replicated, may hold values from -1.25 to 1.25
Outputs:
- features: bfloat16 [128, 16, 256, 1024], P('inline', None, 'xline')
The draws below stay inside these ranges and needn't reach their ends.
Inputs may be any that keep to these rules, and one draw needn't show every extreme that they name: Of one device's 256 traces at most 8 name the same owner, and in every draw some device sends exactly 8 to some owner.
All inputs are finite; a program needn't handle non-finite values.
Results may differ from the reference program's by a relative error of at most 0.0062.
Values may be sent and summed in bfloat16 or wider, within the bound.
No kernel may reach another device: no remote copies, remote signals or barrier semaphores. Data moves between devices by JAX's collectives and lax.ppermute only.
A program may use at most 192 MiB of HBM per device.

```python
import math
import jax
import jax.numpy as jnp
import numpy as np
from jax import lax

SAMPLES = 1024
TR_DEV = 256
CH = 32
OUT_CH = 16
BX = 16
BY = 16
CAP = 8
TRACES = 32768
NBX = 128
NBY = 256
N_XLINE = 16
DEVICES = 128


def plant(array, stream_key, low, high):
    shape = array.shape
    place = [jax.random.randint(jax.random.fold_in(stream_key, axis), (), 0, shape[axis]) for axis in range(len(shape))]
    array = array.at[tuple(place)].set(low)
    longest = shape.index(max(shape))
    place[longest] = (place[longest] + 1) % shape[longest]
    return array.at[tuple(place)].set(high)


def block_levels(stream_key, extent, shards, smallest, top_value):
    def one(dim, parts):
        heights = jax.random.uniform(jax.random.fold_in(jax.random.fold_in(stream_key, 6), dim), (parts,), jnp.float32, smallest / len(shards), top_value / len(shards))
        return jnp.repeat(jnp.exp(heights), extent[dim] // parts).reshape((-1,) + (1,) * (len(extent) - dim - 1))

    gain = one(*shards[0])
    for cut in shards[1:]:
        gain = gain * one(*cut)
    return gain


def deal_out(stream_key, own, number, rows, count, top, bound, skew):
    order = jax.random.permutation(stream_key, count)
    heavy_load, common = load_shares(count, rows * top, bound, skew, True), load_shares(count, rows * top, bound, skew, False)
    places = jnp.arange(count)

    def named(lengths, turn):
        used = int((lengths > 0).sum())
        fixed = max(1, used // 4)
        moved = fixed + (places - fixed + turn * (used - fixed)) % max(1, count - fixed)
        return jnp.zeros((count,), jnp.int32).at[order[jnp.where(places < fixed, places, moved)]].set(jnp.asarray(lengths, jnp.int32))

    lengths = jnp.where(number % 4 == 0, named(heavy_load, number // 4), named(common, number - number // 4 - 1))
    mixed = jax.random.permutation(jax.random.fold_in(own, 3), count)
    donor, receiver = mixed[0:count // 2 * 2:2], mixed[1:count // 2 * 2:2]
    margin = jnp.minimum(lengths[donor] - 1, bound - lengths[receiver]) // 2
    margin = jnp.where((donor == order[0]) | (receiver == order[0]) | (lengths[receiver] == 0), 0, jnp.maximum(margin, 0))
    moved = jax.random.randint(jax.random.fold_in(own, 4), (count // 2,), 0, 1 << 20) % (margin + 1)
    lengths = lengths.at[donor].add(-moved).at[receiver].add(moved)
    items = jnp.searchsorted(jnp.cumsum(lengths), jnp.arange(rows * top), side="right").astype(jnp.int32)
    grid = items.reshape(top, rows).T
    grid = grid[jax.random.permutation(jax.random.fold_in(own, 1), rows)]
    turn = jax.random.randint(jax.random.fold_in(own, 2), (rows, 1), 0, top)
    return jnp.take_along_axis(grid, (jnp.arange(top)[None, :] + turn) % top, axis=1)


def load_shares(number_of, total, limit, slope, full):
    weights = [(1 << 20) // math.isqrt(rank ** slope) + 1 for rank in range(1, number_of + 1)]
    largest = limit if full else min(limit, max(-(-total // number_of), total * weights[0] // sum(weights)))
    least = 1 if total - largest >= number_of - 1 else 0
    holding, rest = [largest] + [least] * (number_of - 1), total - largest - least * (number_of - 1)
    while rest > 0:
        candidates = [i for i in range(1, number_of) if holding[i] < largest] or [i for i in range(1, number_of) if holding[i] < limit]
        whole, remaining = sum([weights[i] for i in candidates]), rest
        for i in candidates:
            extra = min(limit - holding[i], max(1, remaining * weights[i] // whole), rest)
            holding[i] = holding[i] + extra
            rest = rest - extra
    return np.array(holding)


def normal_values(stream_key, dims, spread, most, pieces=(), kind=jnp.bfloat16):
    entries = spread * jax.random.normal(stream_key, dims, jnp.float32)
    if pieces:
        entries = entries * block_levels(stream_key, dims, pieces, -0.22, 0.18)
    return jnp.clip(entries, -most, most).astype(kind)


def setup_inputs(seed: int = 0) -> dict:
    key_of = jax.random.split(jax.random.key(seed), 9)
    traces = normal_values(key_of[0], (TRACES, SAMPLES), 1.0, 6.0, ((0, 128),))
    owner_keys = jax.random.split(jax.random.fold_in(key_of[1], 1), TRACES // TR_DEV)
    owner_turns = jax.random.permutation(jax.random.fold_in(key_of[1], 3), TRACES // TR_DEV)
    owner = jax.vmap(lambda own, number: deal_out(jax.random.fold_in(key_of[1], 2), own, number, TR_DEV, DEVICES, 1, CAP, 2))(owner_keys, owner_turns).reshape((TRACES, 1))
    bin_ids = plant(jax.random.randint(key_of[2], (TRACES,), 0, (BX + 2) * (BY + 2)), jax.random.fold_in(key_of[2], 1), 0, ((BX + 2) * (BY + 2)) - 1).astype(jnp.int32)
    fold = plant(jax.random.randint(key_of[3], (NBX, NBY), 1, 9), jax.random.fold_in(key_of[3], 1), 1, 8).astype(jnp.int32)
    w_first = normal_values(key_of[4], (CH, 3), 3 ** -0.5, 3.5)
    w_second = normal_values(key_of[5], (3, CH, CH), (3 * CH) ** -0.5, 0.625)
    w_noise = normal_values(key_of[6], (CH,), CH ** -0.5, 1.0)
    w_volume = normal_values(key_of[7], (OUT_CH, 27), 27 ** -0.5, 1.25)
    return dict(traces=traces, owner=owner, bin_ids=bin_ids, fold=fold, w_first=w_first, w_second=w_second, w_noise=w_noise, w_volume=w_volume)


def shifted(values, offset):
    if offset == 0:
        return values
    zeros_part = jnp.zeros(values.shape[:-1] + (abs(offset),), values.dtype)
    if offset > 0:
        return jnp.concatenate([values[..., offset:], zeros_part], axis=-1)
    return jnp.concatenate([zeros_part, values[..., :offset]], axis=-1)


def denoise(block, w_first, w_second, w_noise):
    count, samples = block.shape
    channels = w_first.shape[0]
    taps_in = jnp.stack([shifted(block, k - 1) for k in range(3)], 0).reshape(3, count * samples)
    first = jnp.dot(w_first, taps_in, preferred_element_type=jnp.float32)
    hidden = jax.nn.relu(first).astype(jnp.bfloat16).reshape(channels, count, samples)
    total = jnp.zeros((channels, count * samples), jnp.float32)
    for k in range(3):
        moved = shifted(hidden, 4 * (k - 1)).reshape(channels, count * samples)
        total = total + jnp.dot(w_second[k], moved, preferred_element_type=jnp.float32)
    second = jax.nn.relu(total)
    noise = jnp.dot(w_noise.astype(jnp.float32)[None, :], second, precision=lax.Precision.HIGHEST)[0]
    return (block.astype(jnp.float32) - noise.reshape(count, samples)).astype(jnp.bfloat16)


def reference(traces, owner, bin_ids, fold, w_first, w_second, w_noise, w_volume):
    blocks = traces.reshape(TRACES // 256, 256, SAMPLES)
    denoised = lax.map(lambda blk: denoise(blk, w_first, w_second, w_noise), blocks).reshape(TRACES, SAMPLES)
    target = owner[:, 0]
    tile_in = target // N_XLINE
    tile_x = target % N_XLINE
    row_in = bin_ids // (BY + 2)
    col_in = bin_ids % (BY + 2)
    glob_x = tile_in * BX + row_in - 1
    glob_y = tile_x * BY + col_in - 1
    valid = (glob_x >= 0) & (glob_x < NBX) & (glob_y >= 0) & (glob_y < NBY)
    segment = jnp.where(valid, glob_x * NBY + glob_y, NBX * NBY).astype(jnp.int32)
    stack = jax.ops.segment_sum(denoised.astype(jnp.float32), segment, num_segments=NBX * NBY + 1)[:-1]
    stack = stack.reshape(NBX, NBY, SAMPLES)
    volume = (stack / fold[:, :, None].astype(jnp.float32)).astype(jnp.bfloat16)
    padded = jnp.pad(volume, 1)

    def one_row(index):
        window = lax.dynamic_slice_in_dim(padded, index, 3, 0)
        columns = []
        for dx in range(3):
            for dy in range(3):
                for dt in range(3):
                    columns.append(window[dx, dy:dy + NBY, dt:dt + SAMPLES])
        columns = jnp.stack(columns, 0).reshape(27, NBY * SAMPLES)
        result = jnp.dot(w_volume, columns, preferred_element_type=jnp.float32)
        return result.astype(jnp.bfloat16).reshape(OUT_CH, NBY, SAMPLES)

    return lax.map(one_row, jnp.arange(NBX, dtype=jnp.int32))
```

```python
import jax
import jax.numpy as jnp
from jax import lax
from jax.experimental import pallas as pl
from jax.experimental.pallas import tpu as pltpu
from jax.sharding import PartitionSpec as P

F32 = jnp.float32
BF16 = jnp.bfloat16
WIN = 24
PAD = 8
QP = 24
TAIL = 128


def iota(shape, dim):
    return lax.broadcasted_iota(jnp.int32, shape, dim)


def first_weights(w_first):
    shape = (4, 8, 32, 48)
    delta = iota(shape, 3) - 4 * iota(shape, 1) - iota(shape, 0) - 3
    out = jnp.zeros(shape, BF16)
    for k in range(3):
        out = jnp.where(delta == k, w_first[:, k][None, None, :, None], out)
    return out.reshape(1024, 48)


def second_weights(w_second):
    shape = (3, 8, 2, 4, 256)
    step = iota(shape, 4) // 32 - 2 * iota(shape, 0) - iota(shape, 2)
    out = jnp.zeros(shape, BF16)
    for k in range(3):
        wide = jnp.tile(w_second[k], (1, 8)).reshape(8, 4, 256)
        out = jnp.where(step == k, wide[None, :, None], out)
    return out.reshape(192, 256)


def noise_weights(w_noise):
    w = w_noise.astype(F32).reshape(8, 1, 4)
    return jnp.broadcast_to(jnp.broadcast_to(w, (8, 2, 4)).reshape(64, 1), (64, 256))


def volume_weights(w_volume):
    w = w_volume.reshape(16, 3, 3, 3).transpose(0, 1, 3, 2)
    shape = (16, 16, 3, 3, QP)
    delta = iota(shape, 4) - iota(shape, 1)
    out = jnp.zeros(shape, BF16)
    for k in range(3):
        out = jnp.where(delta == k, w[:, None, :, :, k][..., None], out)
    return jnp.pad(out.reshape(256, 9 * QP), ((0, 0), (0, 8)))


def denoise_kernel(x_ref, own_col_ref, own_row_ref, bins_ref, w1_ref, w2_ref, wn_ref, out_ref, xt, dt):
    traces, samples = x_ref.shape
    slots = out_ref.shape[0]
    rows = xt.shape[0]
    xt[0:PAD, :] = jnp.zeros((PAD, traces), F32)
    xt[PAD + samples : rows, :] = jnp.zeros((rows - PAD - samples, traces), F32)
    for k in range(samples // 128):
        xt[PAD + 128 * k : PAD + 128 * (k + 1), :] = x_ref[:, 128 * k : 128 * (k + 1)].astype(F32).T
    windows = -(-samples // WIN)
    sub = iota((3, 8, traces), 1)

    def window(j, low, high):
        start = WIN * j
        if not isinstance(j, int):
            start = pl.multiple_of(start, 8)
        xs = xt[pl.ds(start, 48), :].astype(BF16)
        parts = []
        for p in range(4):
            h = jnp.dot(w1_ref[256 * p : 256 * (p + 1), :], xs, preferred_element_type=F32)
            h = jnp.maximum(h, 0.0).astype(BF16)
            if low or high < 8:
                row = iota((256, traces), 0)
                h = jnp.where((row >= 32 * low) & (row < 32 * high), h, jnp.zeros_like(h))
            o = jnp.dot(w2_ref[...], h, preferred_element_type=F32)
            o = jnp.maximum(o, 0.0).reshape(3, 64, traces) * wn_ref[...][None]
            parts.append(jnp.sum(o.reshape(3, 8, 8, traces), axis=1))
        even = (sub & 1) == 0

        def pair(a, b, shift, mask):
            return jnp.where(mask, a + pltpu.roll(a, 8 - shift, 1), b + pltpu.roll(b, shift, 1))

        lo = pair(parts[0], parts[1], 1, even)
        hi = pair(parts[2], parts[3], 1, even)
        noise = pair(lo, hi, 2, (sub & 2) == 0)
        x = xt[pl.ds(start + PAD, WIN), :]
        dt[pl.ds(start, WIN), :] = x - noise.reshape(WIN, traces)

    window(0, 1, 8)

    def step(j, carry):
        window(j, 0, 8)
        return carry

    lax.fori_loop(1, windows - 1, step, 0)
    last = windows - 1
    window(last, 0, (samples - WIN * last + 4) // 4)

    same = own_col_ref[...] == own_row_ref[...]
    earlier = same & (iota((traces, traces), 0) < iota((traces, traces), 1))
    rank = jnp.sum(jnp.where(earlier, 1.0, 0.0), axis=0, keepdims=True).astype(jnp.int32)
    slot = own_row_ref[...] * 8 + rank
    placing = jnp.where(iota((slots, traces), 0) == slot, 1.0, 0.0).astype(BF16)
    nt = (((1,), (1,)), ((), ()))
    for k in range(samples // 256):
        block = dt[256 * k : 256 * (k + 1), :].astype(BF16)
        out_ref[:, 256 * k : 256 * (k + 1)] = lax.dot_general(
            placing, block, nt, preferred_element_type=F32
        ).astype(BF16)
    which = iota((TAIL, traces), 0)
    row, col = bins_ref[...] // 18 + 1, bins_ref[...] % 18 + 1
    tail = jnp.where(which == 0, row, jnp.where(which == 1, col, 0)).astype(F32).astype(BF16)
    out_ref[:, samples:] = lax.dot_general(placing, tail, nt, preferred_element_type=F32).astype(BF16)


def stack_kernel(recv_ref, fold_ref, main_ref, up_ref, down_ref, cols_ref):
    slots = recv_ref.shape[0]
    blocks, bins, _ = main_ref.shape
    samples = recv_ref.shape[1] - TAIL
    tail = recv_ref[:, samples:].astype(F32).T
    place = ((tail[0:1] - 1.0) * QP + (tail[1:2] - 1.0)).astype(jnp.int32)
    select = jnp.where(iota((bins, slots), 0) == place, 1.0, 0.0).astype(BF16)
    for c in range(0, blocks - 1, 2):
        both = jnp.dot(select, recv_ref[:, 128 * c : 128 * (c + 2)], preferred_element_type=F32)
        main_ref[c] = both[:, :128]
        main_ref[c + 1] = both[:, 128:]
    main_ref[blocks - 1] = fold_ref[...]
    for c in range(blocks):
        lanes = slice(128 * c, 128 * (c + 1))
        up_ref[:, lanes] = main_ref[c, 0 : 2 * QP, :].astype(BF16)
        down_ref[:, lanes] = main_ref[c, bins - 2 * QP : bins, :].astype(BF16)
        for k, q in enumerate((0, 1, 16, 17)):
            cols_ref[c, 24 * k : 24 * k + 18, :] = main_ref[c, pl.ds(q, 18, stride=QP), :]
            cols_ref[c, 24 * k + 18 : 24 * k + 24, :] = jnp.zeros((6, 128), F32)


def columns_kernel(cols_ref, above_ref, below_ref, left_ref, right_ref, acc):
    blocks = cols_ref.shape[0]
    for c in range(blocks):
        acc[:, 128 * c : 128 * (c + 1)] = cols_ref[c]
    above = above_ref[...].astype(F32)
    below = below_ref[...].astype(F32)
    for k, q in enumerate((0, 1, 16, 17)):
        for r in range(2):
            acc[24 * k + r : 24 * k + r + 1, :] += above[r * QP + q : r * QP + q + 1, :]
            acc[24 * k + 16 + r : 24 * k + 17 + r, :] += below[r * QP + q : r * QP + q + 1, :]
    left_ref[...] = acc[0:48, :].astype(BF16)
    right_ref[...] = acc[48:96, :].astype(BF16)


def volume_kernel(main_ref, above_ref, below_ref, left_ref, right_ref, w_ref, out_ref, acc, vs):
    blocks, bins, _ = acc.shape
    samples = 128 * (blocks - 1)
    planes = bins // QP

    @pl.when(pl.program_id(0) == 0)
    def _():
        acc[...] = main_ref[...]
        for c in range(blocks):
            lanes = slice(128 * c, 128 * (c + 1))
            acc[c, 0 : 2 * QP, :] += above_ref[:, lanes].astype(F32)
            acc[c, bins - 2 * QP : bins, :] += below_ref[:, lanes].astype(F32)
            for ref, first in ((left_ref, 0), (right_ref, 16)):
                strip = ref[:, lanes].astype(F32)
                for k in range(2):
                    acc[c, pl.ds(first + k, planes, stride=QP), :] += strip[24 * k : 24 * k + planes, :]
        vs[planes * 3 * QP :, :] = jnp.zeros((8, samples), F32)
        lane = iota((QP, samples), 1)

        def plane(r, carry):
            rows = pl.ds(pl.multiple_of(r * QP, 8), QP)
            fold = acc[blocks - 1, rows, :]
            inside = fold > 0.0
            fold = jnp.where(inside, fold, 1.0)
            v = jnp.concatenate(
                [jnp.where(inside, acc[c, rows, :] / fold, 0.0) for c in range(blocks - 1)], axis=1
            )
            v = v.astype(BF16).astype(F32)
            before = jnp.where(lane == 0, 0.0, pltpu.roll(v, 1, 1))
            after = jnp.where(lane == samples - 1, 0.0, pltpu.roll(v, samples - 1, 1))
            base = r * 3 * QP
            vs[pl.ds(pl.multiple_of(base, 8), QP), :] = before
            vs[pl.ds(pl.multiple_of(base + QP, 8), QP), :] = v
            vs[pl.ds(pl.multiple_of(base + 2 * QP, 8), QP), :] = after
            return carry

        lax.fori_loop(0, planes, plane, 0)

    base = pl.multiple_of(pl.program_id(0) * 3 * QP, 8)
    taps = vs[pl.ds(base, 9 * QP + 8), :].astype(BF16)
    out = jnp.dot(w_ref[...], taps, preferred_element_type=F32)
    out_ref[...] = out.astype(BF16).reshape(out_ref.shape)


def neighbours(first, last, axis):
    size = lax.axis_size(axis)
    up = [(i, i + 1) for i in range(size - 1)]
    down = [(j, i) for i, j in up]
    return lax.ppermute(last, axis, up), lax.ppermute(first, axis, down)


def body(traces, owner, bin_ids, fold, w_first, w_second, w_noise, w_volume):
    devices = lax.axis_size("inline") * lax.axis_size("xline")
    count, samples = traces.shape
    slots = devices * 8
    width = samples + TAIL
    vmem = pl.BlockSpec(memory_space=pltpu.VMEM)
    params = pltpu.CompilerParams(vmem_limit_bytes=56 << 20)
    rows = WIN * (-(-samples // WIN))
    outgoing = pl.pallas_call(
        denoise_kernel,
        out_shape=jax.ShapeDtypeStruct((slots, width), BF16),
        in_specs=[vmem] * 7,
        out_specs=vmem,
        scratch_shapes=[pltpu.VMEM((rows + 32, count), F32), pltpu.VMEM((rows, count), F32)],
        compiler_params=params,
        name="denoise",
    )(
        traces,
        owner,
        owner.reshape(1, count),
        bin_ids.reshape(1, count),
        first_weights(w_first),
        second_weights(w_second),
        noise_weights(w_noise),
    )
    received = lax.all_to_all(
        outgoing.reshape(devices, 8, width), ("inline", "xline"), split_axis=0, concat_axis=0, tiled=True
    ).reshape(slots, width)
    folds = jnp.pad(fold.astype(F32), ((1, 1), (1, QP - 17)))
    folds = jnp.broadcast_to(folds[:, :, None], (18, QP, TAIL)).reshape(18 * QP, TAIL)
    bins = 18 * QP
    main, up, down, cols = pl.pallas_call(
        stack_kernel,
        out_shape=[
            jax.ShapeDtypeStruct((width // 128, bins, 128), F32),
            jax.ShapeDtypeStruct((2 * QP, width), BF16),
            jax.ShapeDtypeStruct((2 * QP, width), BF16),
            jax.ShapeDtypeStruct((width // 128, 96, 128), F32),
        ],
        in_specs=[vmem] * 2,
        out_specs=[vmem] * 4,
        compiler_params=params,
        name="stack",
    )(received, folds)
    above, below = neighbours(up, down, "inline")
    left, right = pl.pallas_call(
        columns_kernel,
        out_shape=[jax.ShapeDtypeStruct((48, width), BF16)] * 2,
        in_specs=[vmem] * 3,
        out_specs=[vmem] * 2,
        scratch_shapes=[pltpu.VMEM((96, width), F32)],
        compiler_params=params,
        name="columns",
    )(cols, above, below)
    from_left, from_right = neighbours(left, right, "xline")
    whole = lambda *shape: pl.BlockSpec(shape, lambda x: (0,) * len(shape))
    return pl.pallas_call(
        volume_kernel,
        out_shape=jax.ShapeDtypeStruct((16, 16, 16, samples), BF16),
        grid=(16,),
        in_specs=[
            whole(width // 128, bins, 128),
            whole(2 * QP, width),
            whole(2 * QP, width),
            whole(48, width),
            whole(48, width),
            whole(256, 9 * QP + 8),
        ],
        out_specs=pl.BlockSpec((1, 16, 16, samples), lambda x: (x, 0, 0, 0)),
        scratch_shapes=[pltpu.VMEM((width // 128, bins, 128), F32), pltpu.VMEM((bins * 3 + 8, samples), F32)],
        compiler_params=params,
        name="volume",
    )(main, above, below, from_left, from_right, volume_weights(w_volume))


def solution(mesh):
    placed = (
        P(("inline", "xline"), None),
        P(("inline", "xline"), None),
        P(("inline", "xline")),
        P("inline", "xline"),
        P(),
        P(),
        P(),
        P(),
    )
    return jax.shard_map(
        body,
        mesh=mesh,
        in_specs=placed,
        out_specs=P("inline", None, "xline", None),
        check_vma=False,
    )
```

```python
import jax
import jax.numpy as jnp
from jax import lax
from jax.experimental import pallas as pl
from jax.experimental.pallas import tpu as pltpu
from jax.sharding import PartitionSpec as P

F32 = jnp.float32
BF16 = jnp.bfloat16
WIN = 24
PAD = 24
QP = 24
TAIL = 128


def iota(shape, dim):
    return lax.broadcasted_iota(jnp.int32, shape, dim)


def picks(shape, row, col):
    return jnp.where(jnp.broadcast_to(row == col, shape), 1.0, 0.0).astype(BF16)


def column(vector, size):
    eye = iota((size, size), 0) == iota((size, size), 1)
    return jnp.sum(jnp.where(eye, vector, 0.0), axis=1, keepdims=True)


def denoise_kernel(x_ref, own_ref, bins_ref, wf_ref, ws_ref, wn_ref, out_ref, xt, dt, ha, hb, w1, w2, wn):
    traces, samples = x_ref.shape
    slots = out_ref.shape[0]
    rows = xt.shape[0]
    windows = -(-samples // WIN)
    hidden_bufs = (ha, hb)

    wf = wf_ref[...].astype(F32)
    taps = [jnp.broadcast_to(column(wf[k : k + 1], 32), (32, 32)) for k in range(3)]
    lane = iota((32, 32), 1)
    for p in range(4):
        for u in range(6):
            block = jnp.zeros((32, 32), F32)
            for k in range(3):
                block = jnp.where(lane == 4 * u + p + k + 3, taps[k], block)
            w1[192 * p + 32 * u : 192 * p + 32 * (u + 1), :] = block.astype(BF16)
    wide = jnp.dot(
        ws_ref[...], picks((32, 256), iota((32, 256), 0), iota((32, 256), 1) % 32), preferred_element_type=F32
    ).astype(BF16)
    row = iota((192, 32), 0)
    channel = picks((192, 32), row % 64 // 8 * 4 + row % 4, iota((192, 32), 1))
    row = iota((192, 256), 0)
    apart = iota((192, 256), 1) // 32 - 2 * (row // 64) - row % 8 // 4
    total = jnp.zeros((192, 256), F32)
    for k in range(3):
        part = jnp.dot(channel, wide[32 * k : 32 * (k + 1)], preferred_element_type=F32)
        total = jnp.where(apart == k, part, total)
    w2[...] = total.astype(BF16)
    row = iota((64, 32), 0)
    of_row = jnp.where(row // 8 * 4 + row % 4 == iota((64, 32), 1), wn_ref[...].astype(F32), 0.0)
    wn[...] = jnp.broadcast_to(jnp.sum(of_row, axis=1, keepdims=True), wn.shape)

    xt[0:PAD, :] = jnp.zeros((PAD, traces), F32)
    xt[PAD + samples : rows, :] = jnp.zeros((rows - PAD - samples, traces), F32)
    for k in range(samples // 128):
        xt[PAD + 128 * k : PAD + 128 * (k + 1), :] = x_ref[:, 128 * k : 128 * (k + 1)].astype(F32).T

    def relu(value):
        return jnp.maximum(value.astype(BF16), jnp.zeros((), BF16))

    def hidden(j, h_ref, before):
        xs = xt[PAD + WIN * j : PAD + WIN * j + 32, :].astype(BF16)
        for p in range(4):
            h_ref[p, 0:64, :] = before[p, 192:256, :]
            h_ref[p, 64:256, :] = relu(
                jnp.dot(w1[192 * p : 192 * (p + 1), :], xs, preferred_element_type=F32)
            )

    sub = iota((3, 8, traces), 1)
    even = (sub & 1) == 0
    low = (sub & 2) == 0

    def pair(a, b, shift, mask):
        return jnp.where(mask, a + pltpu.roll(a, 8 - shift, 1), b + pltpu.roll(b, shift, 1))

    def second(j, h_ref):
        parts = []
        for p in range(4):
            o = jnp.dot(w2[...], h_ref[p], preferred_element_type=F32)
            o = jnp.maximum(o, 0.0).reshape(3, 64, traces) * wn[...][None]
            parts.append(jnp.sum(o.reshape(3, 8, 8, traces), axis=1))
        noise = pair(pair(parts[0], parts[1], 1, even), pair(parts[2], parts[3], 1, even), 2, low)
        x = xt[PAD + WIN * j : PAD + WIN * (j + 1), :]
        dt[WIN * j : WIN * (j + 1), :] = x - noise.reshape(WIN, traces)

    xs = xt[PAD - WIN : PAD - WIN + 32, :].astype(BF16)
    for p in range(4):
        hb[p, 192:224, :] = jnp.zeros((32, traces), BF16)
        hb[p, 224:256, :] = relu(
            jnp.dot(w1[192 * p + 160 : 192 * (p + 1), :], xs, preferred_element_type=F32)
        )
    hidden(0, ha, hb)
    for j in range(windows):
        this, other = hidden_bufs[j % 2], hidden_bufs[1 - j % 2]
        if j + 1 < windows:
            hidden(j + 1, other, this)
        else:
            inside = 32 * ((samples - WIN * j + 4) // 4)
            for p in range(4):
                this[p, inside:, :] = jnp.zeros((256 - inside, traces), BF16)
        second(j, this)

    own = own_ref[...]
    own_col = column(own.astype(F32), traces).astype(jnp.int32)
    earlier = (own_col == own) & (iota((traces, traces), 0) < iota((traces, traces), 1))
    rank = jnp.sum(jnp.where(earlier, 1.0, 0.0), axis=0, keepdims=True).astype(jnp.int32)
    placing = picks((slots, traces), iota((slots, traces), 0), own * 8 + rank)
    nt = (((1,), (1,)), ((), ()))
    for k in range(samples // 256):
        block = dt[256 * k : 256 * (k + 1), :].astype(BF16)
        out_ref[:, 256 * k : 256 * (k + 1)] = lax.dot_general(
            placing, block, nt, preferred_element_type=F32
        ).astype(BF16)
    which = iota((TAIL, traces), 0)
    row, col = bins_ref[...] // 18 + 1, bins_ref[...] % 18 + 1
    tail = jnp.where(which == 0, row, jnp.where(which == 1, col, 0)).astype(F32).astype(BF16)
    out_ref[:, samples:] = lax.dot_general(placing, tail, nt, preferred_element_type=F32).astype(BF16)


def prepare_kernel(fold_ref, wv_ref, fold_out, w_out):
    bins = fold_out.shape[0]
    row = iota((bins, 16), 0)
    of_x = jnp.dot(
        picks((bins, 16), row // QP - 1, iota((bins, 16), 1)),
        fold_ref[...].astype(F32).astype(BF16),
        preferred_element_type=F32,
    )
    own = jnp.sum(jnp.where(row % QP - 1 == iota((bins, 16), 1), of_x, 0.0), axis=1, keepdims=True)
    fold_out[...] = jnp.broadcast_to(own, fold_out.shape)
    cols = w_out.shape[1]
    by_row = jnp.dot(
        picks((256, 16), iota((256, 16), 0) // 16, iota((256, 16), 1)), wv_ref[...], preferred_element_type=F32
    ).astype(BF16)
    col = iota((27, cols), 1)
    tap = col // (3 * QP) * 9 + col // QP % 3
    apart = iota((256, cols), 1) % QP - iota((256, cols), 0) % 16
    total = jnp.zeros((256, cols), F32)
    for k in range(3):
        part = jnp.dot(by_row, picks((27, cols), tap + 3 * k, iota((27, cols), 0)), preferred_element_type=F32)
        total = jnp.where(apart == k, part, total)
    w_out[...] = jnp.where(iota((256, cols), 1) < 9 * QP, total, 0.0).astype(BF16)


def stack_kernel(recv_ref, fold_ref, main_ref, up_ref, down_ref, cols_ref):
    slots = recv_ref.shape[0]
    blocks, bins, _ = main_ref.shape
    samples = recv_ref.shape[1] - TAIL
    tail = recv_ref[:, samples:].astype(F32).T
    place = ((tail[0:1] - 1.0) * QP + (tail[1:2] - 1.0)).astype(jnp.int32)
    select = jnp.where(iota((bins, slots), 0) == place, 1.0, 0.0).astype(BF16)
    for c in range(0, blocks - 1, 2):
        both = jnp.dot(select, recv_ref[:, 128 * c : 128 * (c + 2)], preferred_element_type=F32)
        main_ref[c] = both[:, :128]
        main_ref[c + 1] = both[:, 128:]
    main_ref[blocks - 1] = fold_ref[...]
    for c in range(blocks):
        lanes = slice(128 * c, 128 * (c + 1))
        up_ref[:, lanes] = main_ref[c, 0 : 2 * QP, :].astype(BF16)
        down_ref[:, lanes] = main_ref[c, bins - 2 * QP : bins, :].astype(BF16)
        for k, q in enumerate((0, 1, 16, 17)):
            cols_ref[c, 24 * k : 24 * k + 18, :] = main_ref[c, pl.ds(q, 18, stride=QP), :]
            cols_ref[c, 24 * k + 18 : 24 * k + 24, :] = jnp.zeros((6, 128), F32)


def columns_kernel(cols_ref, above_ref, below_ref, left_ref, right_ref, acc):
    blocks = cols_ref.shape[0]
    for c in range(blocks):
        acc[:, 128 * c : 128 * (c + 1)] = cols_ref[c]
    above = above_ref[...].astype(F32)
    below = below_ref[...].astype(F32)
    for k, q in enumerate((0, 1, 16, 17)):
        for r in range(2):
            acc[24 * k + r : 24 * k + r + 1, :] += above[r * QP + q : r * QP + q + 1, :]
            acc[24 * k + 16 + r : 24 * k + 17 + r, :] += below[r * QP + q : r * QP + q + 1, :]
    left_ref[...] = acc[0:48, :].astype(BF16)
    right_ref[...] = acc[48:96, :].astype(BF16)


def volume_kernel(main_ref, above_ref, below_ref, left_ref, right_ref, w_ref, out_ref, acc, vs):
    blocks, bins, _ = acc.shape
    samples = 128 * (blocks - 1)
    planes = bins // QP

    @pl.when(pl.program_id(0) == 0)
    def _():
        acc[...] = main_ref[...]
        for c in range(blocks):
            lanes = slice(128 * c, 128 * (c + 1))
            acc[c, 0 : 2 * QP, :] += above_ref[:, lanes].astype(F32)
            acc[c, bins - 2 * QP : bins, :] += below_ref[:, lanes].astype(F32)
            for ref, first in ((left_ref, 0), (right_ref, 16)):
                strip = ref[:, lanes].astype(F32)
                for k in range(2):
                    acc[c, pl.ds(first + k, planes, stride=QP), :] += strip[24 * k : 24 * k + planes, :]
        vs[planes * 3 * QP :, :] = jnp.zeros((8, samples), F32)

    lane = iota((QP, samples), 1)

    def plane(r):
        rows = pl.ds(pl.multiple_of(r * QP, 8), QP)
        fold = acc[blocks - 1, rows, :]
        inside = fold > 0.0
        fold = jnp.where(inside, fold, 1.0)
        v = jnp.concatenate(
            [jnp.where(inside, acc[c, rows, :] / fold, 0.0) for c in range(blocks - 1)], axis=1
        )
        v = v.astype(BF16).astype(F32)
        before = jnp.where(lane == 0, 0.0, pltpu.roll(v, 1, 1))
        after = jnp.where(lane == samples - 1, 0.0, pltpu.roll(v, samples - 1, 1))
        base = r * 3 * QP
        vs[pl.ds(pl.multiple_of(base, 8), QP), :] = before
        vs[pl.ds(pl.multiple_of(base + QP, 8), QP), :] = v
        vs[pl.ds(pl.multiple_of(base + 2 * QP, 8), QP), :] = after

    count = out_ref.shape[0]
    at = pl.program_id(0) * count

    @pl.when(pl.program_id(0) == 0)
    def _():
        plane(0)
        plane(1)

    for k in range(count):
        plane(at + 2 + k)
    for k in range(count):
        base = pl.multiple_of((at + k) * 3 * QP, 8)
        taps = vs[pl.ds(base, 9 * QP + 8), :].astype(BF16)
        for c in range(0, samples, 256):
            out = jnp.dot(w_ref[...], taps[:, c : c + 256], preferred_element_type=F32)
            out_ref[k, :, :, c : c + 256] = out.astype(BF16).reshape(16, 16, 256)


def neighbours(first, last, axis):
    size = lax.axis_size(axis)
    up = [(i, i + 1) for i in range(size - 1)]
    down = [(j, i) for i, j in up]
    return lax.ppermute(last, axis, up), lax.ppermute(first, axis, down)


def body(traces, owner, bin_ids, fold, w_first, w_second, w_noise, w_volume):
    devices = lax.axis_size("inline") * lax.axis_size("xline")
    count, samples = traces.shape
    slots = devices * 8
    width = samples + TAIL
    vmem = pl.BlockSpec(memory_space=pltpu.VMEM)
    params = pltpu.CompilerParams(vmem_limit_bytes=24 << 20)
    rows = WIN * (-(-samples // WIN))
    outgoing = pl.pallas_call(
        denoise_kernel,
        out_shape=jax.ShapeDtypeStruct((slots, width), BF16),
        in_specs=[vmem] * 6,
        out_specs=vmem,
        scratch_shapes=[
            pltpu.VMEM((PAD + rows + 8, count), F32),
            pltpu.VMEM((rows, count), F32),
            pltpu.VMEM((4, 256, count), BF16),
            pltpu.VMEM((4, 256, count), BF16),
            pltpu.VMEM((768, 32), BF16),
            pltpu.VMEM((192, 256), BF16),
            pltpu.VMEM((64, count), F32),
        ],
        compiler_params=params,
        name="denoise",
    )(
        traces,
        owner.reshape(1, count),
        bin_ids.reshape(1, count),
        w_first.T,
        w_second.reshape(96, 32),
        w_noise.reshape(1, 32),
    )
    bins = 18 * QP
    folds, w_taps = pl.pallas_call(
        prepare_kernel,
        out_shape=[jax.ShapeDtypeStruct((bins, TAIL), F32), jax.ShapeDtypeStruct((256, 9 * QP + 8), BF16)],
        in_specs=[vmem] * 2,
        out_specs=[vmem] * 2,
        compiler_params=params,
        name="prepare",
    )(fold, w_volume)
    received = lax.all_to_all(
        outgoing.reshape(devices, 8, width), ("inline", "xline"), split_axis=0, concat_axis=0, tiled=True
    ).reshape(slots, width)
    main, up, down, cols = pl.pallas_call(
        stack_kernel,
        out_shape=[
            jax.ShapeDtypeStruct((width // 128, bins, 128), F32),
            jax.ShapeDtypeStruct((2 * QP, width), BF16),
            jax.ShapeDtypeStruct((2 * QP, width), BF16),
            jax.ShapeDtypeStruct((width // 128, 96, 128), F32),
        ],
        in_specs=[vmem] * 2,
        out_specs=[vmem] * 4,
        compiler_params=params,
        name="stack",
    )(received, folds)
    above, below = neighbours(up, down, "inline")
    left, right = pl.pallas_call(
        columns_kernel,
        out_shape=[jax.ShapeDtypeStruct((48, width), BF16)] * 2,
        in_specs=[vmem] * 3,
        out_specs=[vmem] * 2,
        scratch_shapes=[pltpu.VMEM((96, width), F32)],
        compiler_params=params,
        name="columns",
    )(cols, above, below)
    from_left, from_right = neighbours(left, right, "xline")
    whole = lambda *shape: pl.BlockSpec(shape, lambda x: (0,) * len(shape))
    return pl.pallas_call(
        volume_kernel,
        out_shape=jax.ShapeDtypeStruct((16, 16, 16, samples), BF16),
        grid=(8,),
        in_specs=[
            whole(width // 128, bins, 128),
            whole(2 * QP, width),
            whole(2 * QP, width),
            whole(48, width),
            whole(48, width),
            whole(256, 9 * QP + 8),
        ],
        out_specs=pl.BlockSpec((2, 16, 16, samples), lambda x: (x, 0, 0, 0)),
        scratch_shapes=[pltpu.VMEM((width // 128, bins, 128), F32), pltpu.VMEM((bins * 3 + 8, samples), F32)],
        compiler_params=params,
        name="volume",
    )(main, above, below, from_left, from_right, w_taps)


def solution(mesh):
    placed = (
        P(("inline", "xline"), None),
        P(("inline", "xline"), None),
        P(("inline", "xline")),
        P("inline", "xline"),
        P(),
        P(),
        P(),
        P(),
    )
    return jax.shard_map(
        body,
        mesh=mesh,
        in_specs=placed,
        out_specs=P("inline", None, "xline", None),
        check_vma=False,
    )
```

```python
import jax
import jax.numpy as jnp
from jax import lax
from jax.experimental import pallas as pl
from jax.experimental.pallas import tpu as pltpu
from jax.sharding import PartitionSpec as P

F32 = jnp.float32
BF16 = jnp.bfloat16
WIN = 24
PAD = 24
SIDE = 18
BINS = 328
EDGE = 2 * SIDE
STRIP = 40
TAIL = 128


def iota(shape, dim):
    return lax.broadcasted_iota(jnp.int32, shape, dim)


def picks(shape, row, col):
    return jnp.where(jnp.broadcast_to(row == col, shape), 1.0, 0.0).astype(BF16)


def column(vector, size):
    eye = iota((size, size), 0) == iota((size, size), 1)
    return jnp.sum(jnp.where(eye, vector, 0.0), axis=1, keepdims=True)


def denoise_kernel(*refs):
    ins, out_hbm, bufs = refs[:6], refs[6], refs[7:13]
    xt, dt, ha, hb, w1, w2, wn, out_ref, in_sems, out_sems = refs[13:]
    x_ref, own_ref, bins_ref, wf_ref, ws_ref, wn_ref = bufs
    loads = [pltpu.make_async_copy(src, dst, in_sems.at[k]) for k, (src, dst) in enumerate(zip(ins, bufs))]
    for load in loads:
        load.start()
    traces, samples = x_ref.shape
    slots = out_ref.shape[0]
    rows = xt.shape[0]
    windows = -(-samples // WIN)
    hidden_bufs = (ha, hb)

    for load in loads[1:]:
        load.wait()

    own = own_ref[...]
    own_col = column(own.astype(F32), traces).astype(jnp.int32)
    earlier = (own_col == own) & (iota((traces, traces), 0) < iota((traces, traces), 1))
    rank = jnp.sum(jnp.where(earlier, 1.0, 0.0), axis=0, keepdims=True).astype(jnp.int32)
    placing = picks((slots, traces), iota((slots, traces), 0), own * 8 + rank)
    stores = []

    def place(start, width, rows):
        out_ref[:, start : start + width] = lax.dot_general(
            placing, rows, (((1,), (1,)), ((), ())), preferred_element_type=F32
        ).astype(BF16)
        store = pltpu.make_async_copy(
            out_ref.at[:, pl.ds(start, width)], out_hbm.at[:, pl.ds(start, width)], out_sems.at[len(stores)]
        )
        store.start()
        stores.append(store)

    which = iota((TAIL, traces), 0)
    row, col = bins_ref[...] // 18 + 1, bins_ref[...] % 18 + 1
    tail = jnp.where(which == 0, row, jnp.where(which == 1, col, 0)).astype(F32).astype(BF16)
    place(samples, TAIL, tail)

    wf = wf_ref[...].astype(F32)
    taps = [jnp.broadcast_to(column(wf[k : k + 1], 32), (32, 32)) for k in range(3)]
    lane = iota((32, 32), 1)
    for p in range(4):
        for u in range(6):
            block = jnp.zeros((32, 32), F32)
            for k in range(3):
                block = jnp.where(lane == 4 * u + p + k + 3, taps[k], block)
            w1[192 * p + 32 * u : 192 * p + 32 * (u + 1), :] = block.astype(BF16)
    wide = jnp.dot(
        ws_ref[...], picks((32, 256), iota((32, 256), 0), iota((32, 256), 1) % 32), preferred_element_type=F32
    ).astype(BF16)
    row = iota((192, 32), 0)
    channel = picks((192, 32), row % 64 // 8 * 4 + row % 4, iota((192, 32), 1))
    row = iota((192, 256), 0)
    apart = iota((192, 256), 1) // 32 - 2 * (row // 64) - row % 8 // 4
    total = jnp.zeros((192, 256), F32)
    for k in range(3):
        part = jnp.dot(channel, wide[32 * k : 32 * (k + 1)], preferred_element_type=F32)
        total = jnp.where(apart == k, part, total)
    w2[...] = total.astype(BF16)
    row = iota((64, 32), 0)
    of_row = jnp.where(row // 8 * 4 + row % 4 == iota((64, 32), 1), wn_ref[...].astype(F32), 0.0)
    wn[...] = jnp.broadcast_to(jnp.sum(of_row, axis=1, keepdims=True), wn.shape)

    loads[0].wait()
    xt[0:PAD, :] = jnp.zeros((PAD, traces), F32)
    xt[PAD + samples : rows, :] = jnp.zeros((rows - PAD - samples, traces), F32)
    for k in range(samples // 128):
        xt[PAD + 128 * k : PAD + 128 * (k + 1), :] = x_ref[:, 128 * k : 128 * (k + 1)].astype(F32).T

    def relu(value):
        return jnp.maximum(value.astype(BF16), jnp.zeros((), BF16))

    def hidden(j, h_ref, before):
        xs = xt[PAD + WIN * j : PAD + WIN * j + 32, :].astype(BF16)
        for p in range(4):
            h_ref[p, 0:64, :] = before[p, 192:256, :]
            h_ref[p, 64:256, :] = relu(
                jnp.dot(w1[192 * p : 192 * (p + 1), :], xs, preferred_element_type=F32)
            )

    sub = iota((3, 8, traces), 1)
    even = (sub & 1) == 0
    low = (sub & 2) == 0

    def pair(a, b, shift, mask):
        return jnp.where(mask, a + pltpu.roll(a, 8 - shift, 1), b + pltpu.roll(b, shift, 1))

    def second(j, h_ref):
        parts = []
        for p in range(4):
            o = jnp.dot(w2[...], h_ref[p], preferred_element_type=F32)
            o = jnp.maximum(o, 0.0).reshape(3, 64, traces) * wn[...][None]
            parts.append(jnp.sum(o.reshape(3, 8, 8, traces), axis=1))
        noise = pair(pair(parts[0], parts[1], 1, even), pair(parts[2], parts[3], 1, even), 2, low)
        x = xt[PAD + WIN * j : PAD + WIN * (j + 1), :]
        dt[WIN * j : WIN * (j + 1), :] = x - noise.reshape(WIN, traces)

    xs = xt[PAD - WIN : PAD - WIN + 32, :].astype(BF16)
    for p in range(4):
        hb[p, 192:224, :] = jnp.zeros((32, traces), BF16)
        hb[p, 224:256, :] = relu(
            jnp.dot(w1[192 * p + 160 : 192 * (p + 1), :], xs, preferred_element_type=F32)
        )
    hidden(0, ha, hb)
    for j in range(windows):
        this, other = hidden_bufs[j % 2], hidden_bufs[1 - j % 2]
        if j + 1 < windows:
            hidden(j + 1, other, this)
        else:
            inside = 32 * ((samples - WIN * j + 4) // 4)
            for p in range(4):
                this[p, inside:, :] = jnp.zeros((256 - inside, traces), BF16)
        second(j, this)
        while len(stores) - 1 < min(WIN * (j + 1), samples) // 256:
            start = 256 * (len(stores) - 1)
            place(start, 256, dt[start : start + 256, :].astype(BF16))
    for store in stores:
        store.wait()


def prepare_kernel(fold_ref, wv_ref, fold_out, w_out):
    bins = fold_out.shape[0]
    row = iota((bins, 16), 0)
    of_x = jnp.dot(
        picks((bins, 16), row // SIDE - 1, iota((bins, 16), 1)),
        fold_ref[...].astype(F32).astype(BF16),
        preferred_element_type=F32,
    )
    own = jnp.sum(jnp.where(row % SIDE - 1 == iota((bins, 16), 1), of_x, 0.0), axis=1, keepdims=True)
    fold_out[...] = jnp.broadcast_to(own, fold_out.shape)
    rows, cols = w_out.shape
    by_row = jnp.dot(
        picks((rows, 16), iota((rows, 16), 0) // 16 % 16, iota((rows, 16), 1)),
        wv_ref[...],
        preferred_element_type=F32,
    ).astype(BF16)
    row, col = iota((rows, cols), 0), iota((rows, cols), 1)
    dx = col // SIDE % 4 - row // 256
    dy = col % SIDE - row % 16
    near = (dx >= 0) & (dx < 3)
    dt = iota((27, cols), 1) // (4 * SIDE)
    total = jnp.zeros((rows, cols), F32)
    for k in range(9):
        taps = picks((27, cols), 3 * k + dt, iota((27, cols), 0))
        part = jnp.dot(by_row, taps, preferred_element_type=F32)
        total = jnp.where(near & (dx == k // 3) & (dy == k % 3), part, total)
    w_out[...] = total.astype(BF16)


def stack_kernel(recv_ref, fold_ref, main_ref, up_ref, down_ref, cols_ref):
    slots = recv_ref.shape[0]
    blocks, bins, _ = main_ref.shape
    samples = recv_ref.shape[1] - TAIL
    tail = recv_ref[:, samples:].astype(F32).T
    place = ((tail[0:1] - 1.0) * SIDE + (tail[1:2] - 1.0)).astype(jnp.int32)
    select = picks((bins, slots), iota((bins, slots), 0), place)
    for c in range(0, blocks - 1, 2):
        both = jnp.dot(select, recv_ref[:, 128 * c : 128 * (c + 2)], preferred_element_type=F32)
        main_ref[c] = both[:, :128]
        main_ref[c + 1] = both[:, 128:]
    main_ref[blocks - 1] = fold_ref[...]
    edge = iota((STRIP, 128), 0) < EDGE
    for c in range(blocks):
        lanes = slice(128 * c, 128 * (c + 1))
        up_ref[:, lanes] = jnp.where(edge, main_ref[c, 0:STRIP, :], 0.0).astype(BF16)
        down_ref[:, lanes] = main_ref[c, bins - STRIP : bins, :].astype(BF16)
        for k, q in enumerate((0, 1, 16, 17)):
            cols_ref[c, 24 * k : 24 * k + SIDE, :] = main_ref[c, pl.ds(q, SIDE, stride=SIDE), :]
            cols_ref[c, 24 * k + SIDE : 24 * (k + 1), :] = jnp.zeros((24 - SIDE, 128), F32)


def columns_kernel(cols_ref, above_ref, below_ref, left_ref, right_ref, acc):
    blocks = cols_ref.shape[0]
    for c in range(blocks):
        acc[:, 128 * c : 128 * (c + 1)] = cols_ref[c]
    above = above_ref[...].astype(F32)
    below = below_ref[...].astype(F32)
    for k, q in enumerate((0, 1, 16, 17)):
        for r in range(2):
            at = r * SIDE + q
            acc[24 * k + r : 24 * k + r + 1, :] += above[at : at + 1, :]
            acc[24 * k + 16 + r : 24 * k + 17 + r, :] += below[at : at + 1, :]
    left_ref[...] = acc[0:48, :].astype(BF16)
    right_ref[...] = acc[48:96, :].astype(BF16)


def volume_kernel(main_ref, above_ref, below_ref, left_ref, right_ref, w_ref, out_hbm, acc, vs, out, sems):
    blocks, bins, _ = acc.shape
    samples = 128 * (blocks - 1)
    acc[...] = main_ref[...]
    for c in range(blocks):
        lanes = slice(128 * c, 128 * (c + 1))
        acc[c, 0:STRIP, :] += above_ref[:, lanes].astype(F32)
        acc[c, bins - STRIP : bins, :] += below_ref[:, lanes].astype(F32)
        for ref, first in ((left_ref, 0), (right_ref, 16)):
            strip = ref[:, lanes].astype(F32)
            for k in range(2):
                acc[c, pl.ds(first + k, SIDE, stride=SIDE), :] += strip[24 * k : 24 * k + SIDE, :]

    def taps_of(start, stop):
        lane = iota((stop - start, samples), 1)
        fold = acc[blocks - 1, start:stop, :]
        inside = fold > 0.0
        fold = jnp.where(inside, fold, 1.0)
        v = jnp.concatenate(
            [jnp.where(inside, acc[c, start:stop, :] / fold, 0.0) for c in range(blocks - 1)], axis=1
        )
        v = v.astype(BF16).astype(F32)
        vs[0, start:stop, :] = jnp.where(lane == 0, 0.0, pltpu.roll(v, 1, 1))
        vs[1, start:stop, :] = v
        vs[2, start:stop, :] = jnp.where(lane == samples - 1, 0.0, pltpu.roll(v, samples - 1, 1))

    done, slots = 0, out.shape[0]
    stores = []
    for m in range(8):
        first, last = EDGE * m, EDGE * m + 2 * EDGE
        needed = min(bins, -(-last // 8) * 8)
        taps_of(done, needed)
        done = needed
        taps = jnp.concatenate([vs[dt, first:last, :] for dt in range(3)], axis=0).astype(BF16)
        if m >= slots:
            stores[m - slots].wait()
        for c in range(0, samples, 256):
            part = jnp.dot(w_ref[...], taps[:, c : c + 256], preferred_element_type=F32)
            out[m % slots, :, :, :, c : c + 256] = part.astype(BF16).reshape(2, 16, 16, 256)
        store = pltpu.make_async_copy(
            out.at[m % slots], out_hbm.at[pl.ds(2 * m, 2)], sems.at[m % slots]
        )
        store.start()
        stores.append(store)
    for store in stores[8 - slots :]:
        store.wait()


def neighbours(first, last, axis):
    size = lax.axis_size(axis)
    up = [(i, i + 1) for i in range(size - 1)]
    down = [(j, i) for i, j in up]
    return lax.ppermute(last, axis, up), lax.ppermute(first, axis, down)


def body(traces, owner, bin_ids, fold, w_first, w_second, w_noise, w_volume):
    devices = lax.axis_size("inline") * lax.axis_size("xline")
    count, samples = traces.shape
    slots = devices * 8
    width = samples + TAIL
    vmem = pl.BlockSpec(memory_space=pltpu.VMEM)
    hbm = pl.BlockSpec(memory_space=pltpu.HBM)
    params = pltpu.CompilerParams(vmem_limit_bytes=24 << 20)
    rows = WIN * (-(-samples // WIN))
    outgoing = pl.pallas_call(
        denoise_kernel,
        out_shape=jax.ShapeDtypeStruct((slots, width), BF16),
        in_specs=[hbm] * 6,
        out_specs=hbm,
        scratch_shapes=[
            pltpu.VMEM((count, samples), BF16),
            pltpu.VMEM((1, count), jnp.int32),
            pltpu.VMEM((1, count), jnp.int32),
            pltpu.VMEM((3, 32), BF16),
            pltpu.VMEM((96, 32), BF16),
            pltpu.VMEM((1, 32), BF16),
            pltpu.VMEM((PAD + rows + 8, count), F32),
            pltpu.VMEM((rows, count), F32),
            pltpu.VMEM((4, 256, count), BF16),
            pltpu.VMEM((4, 256, count), BF16),
            pltpu.VMEM((768, 32), BF16),
            pltpu.VMEM((192, 256), BF16),
            pltpu.VMEM((64, count), F32),
            pltpu.VMEM((slots, width), BF16),
            pltpu.SemaphoreType.DMA((6,)),
            pltpu.SemaphoreType.DMA((samples // 256 + 1,)),
        ],
        compiler_params=pltpu.CompilerParams(vmem_limit_bytes=60 << 20),
        name="denoise",
    )(
        traces,
        owner.reshape(1, count),
        bin_ids.reshape(1, count),
        w_first.T,
        w_second.reshape(96, 32),
        w_noise.reshape(1, 32),
    )
    bins = BINS
    folds, w_taps = pl.pallas_call(
        prepare_kernel,
        out_shape=[jax.ShapeDtypeStruct((bins, TAIL), F32), jax.ShapeDtypeStruct((512, 12 * SIDE), BF16)],
        in_specs=[vmem] * 2,
        out_specs=[vmem] * 2,
        compiler_params=params,
        name="prepare",
    )(fold, w_volume)
    received = lax.all_to_all(
        outgoing.reshape(devices, 8, width), ("inline", "xline"), split_axis=0, concat_axis=0, tiled=True
    ).reshape(slots, width)
    main, up, down, cols = pl.pallas_call(
        stack_kernel,
        out_shape=[
            jax.ShapeDtypeStruct((width // 128, bins, 128), F32),
            jax.ShapeDtypeStruct((STRIP, width), BF16),
            jax.ShapeDtypeStruct((STRIP, width), BF16),
            jax.ShapeDtypeStruct((width // 128, 96, 128), F32),
        ],
        in_specs=[vmem] * 2,
        out_specs=[vmem] * 4,
        compiler_params=params,
        name="stack",
    )(received, folds)
    above, below = neighbours(up, down, "inline")
    left, right = pl.pallas_call(
        columns_kernel,
        out_shape=[jax.ShapeDtypeStruct((48, width), BF16)] * 2,
        in_specs=[vmem] * 3,
        out_specs=[vmem] * 2,
        scratch_shapes=[pltpu.VMEM((96, width), F32)],
        compiler_params=params,
        name="columns",
    )(cols, above, below)
    from_left, from_right = neighbours(left, right, "xline")
    return pl.pallas_call(
        volume_kernel,
        out_shape=jax.ShapeDtypeStruct((16, 16, 16, samples), BF16),
        in_specs=[vmem] * 6,
        out_specs=hbm,
        scratch_shapes=[
            pltpu.VMEM((width // 128, bins, 128), F32),
            pltpu.VMEM((3, bins, samples), F32),
            pltpu.VMEM((3, 2, 16, 16, samples), BF16),
            pltpu.SemaphoreType.DMA((3,)),
        ],
        compiler_params=params,
        name="volume",
    )(main, above, below, from_left, from_right, w_taps)


def solution(mesh):
    placed = (
        P(("inline", "xline"), None),
        P(("inline", "xline"), None),
        P(("inline", "xline")),
        P("inline", "xline"),
        P(),
        P(),
        P(),
        P(),
    )
    return jax.shard_map(
        body,
        mesh=mesh,
        in_specs=placed,
        out_specs=P("inline", None, "xline", None),
        check_vma=False,
    )
```

```python
import jax
import jax.numpy as jnp
from jax import lax
from jax.experimental import pallas as pl
from jax.experimental.pallas import tpu as pltpu
from jax.sharding import PartitionSpec as P

F32 = jnp.float32
BF16 = jnp.bfloat16
WIN = 24
PAD = 24
SIDE = 18
BINS = 328
EDGE = 2 * SIDE
STRIP = 40
TAIL = 128


def iota(shape, dim):
    return lax.broadcasted_iota(jnp.int32, shape, dim)


def picks(shape, row, col):
    return jnp.where(jnp.broadcast_to(row == col, shape), 1.0, 0.0).astype(BF16)


def column(vector, size):
    eye = iota((size, size), 0) == iota((size, size), 1)
    return jnp.sum(jnp.where(eye, vector, 0.0), axis=1, keepdims=True)


def denoise_kernel(*refs):
    ins, out_hbm, bufs = refs[:6], refs[6], refs[7:13]
    xt, dt, ha, hb, w1, w2, wn, out_ref, in_sems, out_sems = refs[13:]
    x_ref, own_ref, bins_ref, wf_ref, ws_ref, wn_ref = bufs
    loads = [pltpu.make_async_copy(src, dst, in_sems.at[k]) for k, (src, dst) in enumerate(zip(ins, bufs))]
    for load in loads:
        load.start()
    traces, samples = x_ref.shape
    slots = out_ref.shape[0]
    rows = xt.shape[0]
    windows = -(-samples // WIN)
    hidden_bufs = (ha, hb)

    for load in loads[1:]:
        load.wait()

    own = own_ref[...]
    own_col = column(own.astype(F32), traces).astype(jnp.int32)
    earlier = (own_col == own) & (iota((traces, traces), 0) < iota((traces, traces), 1))
    rank = jnp.sum(jnp.where(earlier, 1.0, 0.0), axis=0, keepdims=True).astype(jnp.int32)
    placing = picks((slots, traces), iota((slots, traces), 0), own * 8 + rank)
    stores = []

    def place(start, width, rows):
        out_ref[:, start : start + width] = lax.dot_general(
            placing, rows, (((1,), (1,)), ((), ())), preferred_element_type=F32
        ).astype(BF16)
        store = pltpu.make_async_copy(
            out_ref.at[:, pl.ds(start, width)], out_hbm.at[:, pl.ds(start, width)], out_sems.at[len(stores)]
        )
        store.start()
        stores.append(store)

    which = iota((TAIL, traces), 0)
    row, col = bins_ref[...] // 18 + 1, bins_ref[...] % 18 + 1
    tail = jnp.where(which == 0, row, jnp.where(which == 1, col, 0)).astype(F32).astype(BF16)
    place(samples, TAIL, tail)

    wf = wf_ref[...].astype(F32)
    taps = [jnp.broadcast_to(column(wf[k : k + 1], 32), (32, 32)) for k in range(3)]
    lane = iota((32, 32), 1)
    for p in range(4):
        for u in range(6):
            block = jnp.zeros((32, 32), F32)
            for k in range(3):
                block = jnp.where(lane == 4 * u + p + k + 3, taps[k], block)
            w1[192 * p + 32 * u : 192 * p + 32 * (u + 1), :] = block.astype(BF16)
    wide = jnp.dot(
        ws_ref[...], picks((32, 256), iota((32, 256), 0), iota((32, 256), 1) % 32), preferred_element_type=F32
    ).astype(BF16)
    row = iota((192, 32), 0)
    channel = picks((192, 32), row % 64 // 8 * 4 + row % 4, iota((192, 32), 1))
    row = iota((192, 256), 0)
    apart = iota((192, 256), 1) // 32 - 2 * (row // 64) - row % 8 // 4
    total = jnp.zeros((192, 256), F32)
    for k in range(3):
        part = jnp.dot(channel, wide[32 * k : 32 * (k + 1)], preferred_element_type=F32)
        total = jnp.where(apart == k, part, total)
    w2[...] = total.astype(BF16)
    row = iota((64, 32), 0)
    of_row = jnp.where(row // 8 * 4 + row % 4 == iota((64, 32), 1), wn_ref[...].astype(F32), 0.0)
    wn[...] = jnp.broadcast_to(jnp.sum(of_row, axis=1, keepdims=True), wn.shape)

    loads[0].wait()
    xt[0:PAD, :] = jnp.zeros((PAD, traces), F32)
    xt[PAD + samples : rows, :] = jnp.zeros((rows - PAD - samples, traces), F32)
    for k in range(samples // 128):
        xt[PAD + 128 * k : PAD + 128 * (k + 1), :] = x_ref[:, 128 * k : 128 * (k + 1)].astype(F32).T

    def relu(value):
        return jnp.maximum(value.astype(BF16), jnp.zeros((), BF16))

    def hidden(j, h_ref, before):
        xs = xt[PAD + WIN * j : PAD + WIN * j + 32, :].astype(BF16)
        for p in range(4):
            h_ref[p, 0:64, :] = before[p, 192:256, :]
            h_ref[p, 64:256, :] = relu(
                jnp.dot(w1[192 * p : 192 * (p + 1), :], xs, preferred_element_type=F32)
            )

    sub = iota((3, 8, traces), 1)
    even = (sub & 1) == 0
    low = (sub & 2) == 0

    def pair(a, b, shift, mask):
        return jnp.where(mask, a + pltpu.roll(a, 8 - shift, 1), b + pltpu.roll(b, shift, 1))

    def second(j, h_ref):
        parts = []
        for p in range(4):
            o = jnp.dot(w2[...], h_ref[p], preferred_element_type=F32)
            o = jnp.maximum(o, 0.0).reshape(3, 64, traces) * wn[...][None]
            parts.append(jnp.sum(o.reshape(3, 8, 8, traces), axis=1))
        noise = pair(pair(parts[0], parts[1], 1, even), pair(parts[2], parts[3], 1, even), 2, low)
        x = xt[PAD + WIN * j : PAD + WIN * (j + 1), :]
        dt[WIN * j : WIN * (j + 1), :] = x - noise.reshape(WIN, traces)

    xs = xt[PAD - WIN : PAD - WIN + 32, :].astype(BF16)
    for p in range(4):
        hb[p, 192:224, :] = jnp.zeros((32, traces), BF16)
        hb[p, 224:256, :] = relu(
            jnp.dot(w1[192 * p + 160 : 192 * (p + 1), :], xs, preferred_element_type=F32)
        )
    hidden(0, ha, hb)
    for j in range(windows):
        this, other = hidden_bufs[j % 2], hidden_bufs[1 - j % 2]
        if j + 1 < windows:
            hidden(j + 1, other, this)
        else:
            inside = 32 * ((samples - WIN * j + 4) // 4)
            for p in range(4):
                this[p, inside:, :] = jnp.zeros((256 - inside, traces), BF16)
        second(j, this)
        while len(stores) - 1 < min(WIN * (j + 1), samples) // 256:
            start = 256 * (len(stores) - 1)
            place(start, 256, dt[start : start + 256, :].astype(BF16))
    for store in stores:
        store.wait()


def prepare_kernel(fold_ref, wv_ref, fold_out, w_out):
    bins = fold_out.shape[0]
    row = iota((bins, 16), 0)
    of_x = jnp.dot(
        picks((bins, 16), row // SIDE - 1, iota((bins, 16), 1)),
        fold_ref[...].astype(F32).astype(BF16),
        preferred_element_type=F32,
    )
    own = jnp.sum(jnp.where(row % SIDE - 1 == iota((bins, 16), 1), of_x, 0.0), axis=1, keepdims=True)
    fold_out[...] = jnp.broadcast_to(own, fold_out.shape)
    rows, cols = w_out.shape
    by_row = jnp.dot(
        picks((rows, 16), iota((rows, 16), 0) // 16 % 16, iota((rows, 16), 1)),
        wv_ref[...],
        preferred_element_type=F32,
    ).astype(BF16)
    row, col = iota((rows, cols), 0), iota((rows, cols), 1)
    dx = col // SIDE % 4 - row // 256
    dy = col % SIDE - row % 16
    near = (dx >= 0) & (dx < 3)
    dt = iota((27, cols), 1) // (4 * SIDE)
    total = jnp.zeros((rows, cols), F32)
    for k in range(9):
        taps = picks((27, cols), 3 * k + dt, iota((27, cols), 0))
        part = jnp.dot(by_row, taps, preferred_element_type=F32)
        total = jnp.where(near & (dx == k // 3) & (dy == k % 3), part, total)
    w_out[...] = total.astype(BF16)


def stack_kernel(recv_ref, fold_ref, main_ref, left_ref, right_ref):
    slots = recv_ref.shape[0]
    blocks, bins, _ = main_ref.shape
    samples = recv_ref.shape[1] - TAIL
    tail = recv_ref[:, samples:].astype(F32).T
    place = ((tail[0:1] - 1.0) * SIDE + (tail[1:2] - 1.0)).astype(jnp.int32)
    select = picks((bins, slots), iota((bins, slots), 0), place)
    for c in range(0, blocks - 1, 2):
        both = jnp.dot(select, recv_ref[:, 128 * c : 128 * (c + 2)], preferred_element_type=F32)
        main_ref[c] = both[:, :128]
        main_ref[c + 1] = both[:, 128:]
    main_ref[blocks - 1] = fold_ref[...]
    pad = jnp.zeros((24 - SIDE, 128), F32)
    for c in range(blocks):
        lanes = slice(128 * c, 128 * (c + 1))
        for ref, first in ((left_ref, 0), (right_ref, 16)):
            cols = [main_ref[c, pl.ds(first + k, SIDE, stride=SIDE), :] for k in range(2)]
            ref[:, lanes] = jnp.concatenate([cols[0], pad, cols[1], pad], axis=0).astype(BF16)


def edges_kernel(main_ref, left_ref, right_ref, up_ref, down_ref, up, down):
    blocks, bins, _ = main_ref.shape
    for c in range(blocks):
        lanes = slice(128 * c, 128 * (c + 1))
        up[:, lanes] = main_ref[c, 0:STRIP, :]
        down[:, lanes] = main_ref[c, bins - STRIP : bins, :]
    for ref, first in ((left_ref, 0), (right_ref, 16)):
        strip = ref[...].astype(F32)
        for k in range(2):
            for r in range(2):
                at = r * SIDE + first + k
                up[at : at + 1, :] += strip[24 * k + r : 24 * k + r + 1, :]
                down[at : at + 1, :] += strip[24 * k + 16 + r : 24 * k + 17 + r, :]
    up_ref[...] = jnp.where(iota(up.shape, 0) < EDGE, up[...], 0.0).astype(BF16)
    down_ref[...] = down[...].astype(BF16)


def add_sides(acc, left_ref, right_ref, start, count):
    for c in range(acc.shape[0]):
        lanes = slice(128 * c, 128 * (c + 1))
        for ref, first in ((left_ref, 0), (right_ref, 16)):
            strip = ref[:, lanes].astype(F32)
            for k in range(2):
                rows = pl.ds(start * SIDE + first + k, count, stride=SIDE)
                acc[c, rows, :] += strip[24 * k + start : 24 * k + start + count, :]


def make_taps(acc, vs, start, stop):
    blocks = acc.shape[0]
    samples = 128 * (blocks - 1)
    lane = iota((stop - start, samples), 1)
    fold = acc[blocks - 1, start:stop, :]
    inside = fold > 0.0
    fold = jnp.where(inside, fold, 1.0)
    v = jnp.concatenate([jnp.where(inside, acc[c, start:stop, :] / fold, 0.0) for c in range(blocks - 1)], axis=1)
    v = v.astype(BF16).astype(F32)
    vs[0, start:stop, :] = jnp.where(lane == 0, 0.0, pltpu.roll(v, 1, 1))
    vs[1, start:stop, :] = v
    vs[2, start:stop, :] = jnp.where(lane == samples - 1, 0.0, pltpu.roll(v, samples - 1, 1))


def convolve(m, vs, w_ref, block):
    taps = jnp.concatenate([vs[dt, EDGE * m : EDGE * (m + 2), :] for dt in range(3)], axis=0).astype(BF16)
    for c in range(0, vs.shape[2], 256):
        part = jnp.dot(w_ref[...], taps[:, c : c + 256], preferred_element_type=F32)
        block[:, :, :, c : c + 256] = part.astype(BF16).reshape(2, 16, 16, 256)


def inner_kernel(main_ref, left_ref, right_ref, w_ref, out_hbm, acc, vs, out, sems):
    acc[...] = main_ref[...]
    add_sides(acc, left_ref, right_ref, 2, 14)
    done, slots = EDGE // 8 * 8, out.shape[0]
    stores = []
    for m in range(1, 7):
        needed = EDGE * (m + 2) // 8 * 8 + 8 * (EDGE * (m + 2) % 8 > 0)
        make_taps(acc, vs, done, needed)
        done = needed
        k = m - 1
        if k >= slots:
            stores[k - slots].wait()
        convolve(m, vs, w_ref, out.at[k % slots])
        store = pltpu.make_async_copy(out.at[k % slots], out_hbm.at[pl.ds(2 * m, 2)], sems.at[k % slots])
        store.start()
        stores.append(store)
    for store in stores[6 - slots :]:
        store.wait()


def outer_kernel(main_ref, left_ref, right_ref, above_ref, below_ref, w_ref, _, out_hbm, acc, vs, out, sems):
    blocks, bins, _ = acc.shape
    top, bottom = 2 * EDGE, (bins - 2 * EDGE) // 8 * 8 - 8
    for c in range(blocks):
        lanes = slice(128 * c, 128 * (c + 1))
        acc[c, 0:top, :] = main_ref[c, 0:top, :]
        acc[c, bottom:bins, :] = main_ref[c, bottom:bins, :]
        acc[c, 0:STRIP, :] += above_ref[:, lanes].astype(F32)
        acc[c, bins - STRIP : bins, :] += below_ref[:, lanes].astype(F32)
    stores = []
    for k, (m, start, stop, row) in enumerate(((0, 0, top, 0), (7, bottom, bins, 14))):
        add_sides(acc, left_ref, right_ref, row, 4)
        make_taps(acc, vs, start, stop)
        convolve(m, vs, w_ref, out.at[k])
        store = pltpu.make_async_copy(out.at[k], out_hbm.at[pl.ds(2 * m, 2)], sems.at[k])
        store.start()
        stores.append(store)
    for store in stores:
        store.wait()


def neighbours(first, last, axis):
    size = lax.axis_size(axis)
    up = [(i, i + 1) for i in range(size - 1)]
    down = [(j, i) for i, j in up]
    return lax.ppermute(last, axis, up), lax.ppermute(first, axis, down)


def body(traces, owner, bin_ids, fold, w_first, w_second, w_noise, w_volume):
    devices = lax.axis_size("inline") * lax.axis_size("xline")
    count, samples = traces.shape
    slots = devices * 8
    width = samples + TAIL
    vmem = pl.BlockSpec(memory_space=pltpu.VMEM)
    hbm = pl.BlockSpec(memory_space=pltpu.HBM)
    params = pltpu.CompilerParams(vmem_limit_bytes=24 << 20)
    rows = WIN * (-(-samples // WIN))
    outgoing = pl.pallas_call(
        denoise_kernel,
        out_shape=jax.ShapeDtypeStruct((slots, width), BF16),
        in_specs=[hbm] * 6,
        out_specs=hbm,
        scratch_shapes=[
            pltpu.VMEM((count, samples), BF16),
            pltpu.VMEM((1, count), jnp.int32),
            pltpu.VMEM((1, count), jnp.int32),
            pltpu.VMEM((3, 32), BF16),
            pltpu.VMEM((96, 32), BF16),
            pltpu.VMEM((1, 32), BF16),
            pltpu.VMEM((PAD + rows + 8, count), F32),
            pltpu.VMEM((rows, count), F32),
            pltpu.VMEM((4, 256, count), BF16),
            pltpu.VMEM((4, 256, count), BF16),
            pltpu.VMEM((768, 32), BF16),
            pltpu.VMEM((192, 256), BF16),
            pltpu.VMEM((64, count), F32),
            pltpu.VMEM((slots, width), BF16),
            pltpu.SemaphoreType.DMA((6,)),
            pltpu.SemaphoreType.DMA((samples // 256 + 1,)),
        ],
        compiler_params=pltpu.CompilerParams(vmem_limit_bytes=60 << 20),
        name="denoise",
    )(
        traces,
        owner.reshape(1, count),
        bin_ids.reshape(1, count),
        w_first.T,
        w_second.reshape(96, 32),
        w_noise.reshape(1, 32),
    )
    bins = BINS
    folds, w_taps = pl.pallas_call(
        prepare_kernel,
        out_shape=[jax.ShapeDtypeStruct((bins, TAIL), F32), jax.ShapeDtypeStruct((512, 12 * SIDE), BF16)],
        in_specs=[vmem] * 2,
        out_specs=[vmem] * 2,
        compiler_params=params,
        name="prepare",
    )(fold, w_volume)
    received = lax.all_to_all(
        outgoing.reshape(devices, 8, width), ("inline", "xline"), split_axis=0, concat_axis=0, tiled=True
    ).reshape(slots, width)
    strip = jax.ShapeDtypeStruct((48, width), BF16)
    edge = jax.ShapeDtypeStruct((STRIP, width), BF16)
    main, left, right = pl.pallas_call(
        stack_kernel,
        out_shape=[jax.ShapeDtypeStruct((width // 128, bins, 128), F32), strip, strip],
        in_specs=[vmem] * 2,
        out_specs=[vmem] * 3,
        compiler_params=params,
        name="stack",
    )(received, folds)
    from_left, from_right = neighbours(left, right, "xline")
    up, down = pl.pallas_call(
        edges_kernel,
        out_shape=[edge, edge],
        in_specs=[vmem] * 3,
        out_specs=[vmem] * 2,
        scratch_shapes=[pltpu.VMEM((STRIP, width), F32)] * 2,
        compiler_params=params,
        name="edges",
    )(main, from_left, from_right)
    above, below = neighbours(up, down, "inline")

    def scratch(slots):
        return [
            pltpu.VMEM((width // 128, bins, 128), F32),
            pltpu.VMEM((3, bins, samples), F32),
            pltpu.VMEM((slots, 2, 16, 16, samples), BF16),
            pltpu.SemaphoreType.DMA((slots,)),
        ]

    features = jax.ShapeDtypeStruct((16, 16, 16, samples), BF16)
    inner = pl.pallas_call(
        inner_kernel,
        out_shape=features,
        in_specs=[vmem] * 4,
        out_specs=hbm,
        scratch_shapes=scratch(3),
        compiler_params=params,
        cost_estimate=pl.CostEstimate(flops=1 << 32, transcendentals=0, bytes_accessed=8 << 20),
        name="inner",
    )(main, from_left, from_right, w_taps)
    return pl.pallas_call(
        outer_kernel,
        out_shape=features,
        in_specs=[vmem] * 6 + [hbm],
        out_specs=hbm,
        scratch_shapes=scratch(2),
        input_output_aliases={6: 0},
        compiler_params=params,
        name="outer",
    )(main, from_left, from_right, above, below, w_taps, inner)


def solution(mesh):
    placed = (
        P(("inline", "xline"), None),
        P(("inline", "xline"), None),
        P(("inline", "xline")),
        P("inline", "xline"),
        P(),
        P(),
        P(),
        P(),
    )
    return jax.shard_map(
        body,
        mesh=mesh,
        in_specs=placed,
        out_specs=P("inline", None, "xline", None),
        check_vma=False,
    )
```

```python
import jax
import jax.numpy as jnp
from jax import lax
from jax.experimental import pallas as pl
from jax.experimental.pallas import tpu as pltpu
from jax.sharding import PartitionSpec as P

F32 = jnp.float32
BF16 = jnp.bfloat16
WIN = 24
PAD = 24
SIDE = 18
BINS = 328
EDGE = 2 * SIDE
STRIP = 40
TAIL = 128


def iota(shape, dim):
    return lax.broadcasted_iota(jnp.int32, shape, dim)


def picks(shape, row, col):
    return jnp.where(jnp.broadcast_to(row == col, shape), 1.0, 0.0).astype(BF16)


def column(vector, size):
    eye = iota((size, size), 0) == iota((size, size), 1)
    return jnp.sum(jnp.where(eye, vector, 0.0), axis=1, keepdims=True)


def denoise_kernel(*refs):
    ins, out_hbm, bufs = refs[:6], refs[6], refs[7:13]
    xt, dt, ha, hb, w1, w2, wn, out_ref, in_sems, out_sems = refs[13:]
    x_ref, own_ref, bins_ref, wf_ref, ws_ref, wn_ref = bufs
    loads = [pltpu.make_async_copy(src, dst, in_sems.at[k]) for k, (src, dst) in enumerate(zip(ins, bufs))]
    for load in loads:
        load.start()
    traces, samples = x_ref.shape
    slots = out_ref.shape[0]
    rows = xt.shape[0]
    windows = -(-samples // WIN)
    hidden_bufs = (ha, hb)

    for load in loads[1:]:
        load.wait()

    own = own_ref[...]
    own_col = column(own.astype(F32), traces).astype(jnp.int32)
    earlier = (own_col == own) & (iota((traces, traces), 0) < iota((traces, traces), 1))
    rank = jnp.sum(jnp.where(earlier, 1.0, 0.0), axis=0, keepdims=True).astype(jnp.int32)
    placing = picks((slots, traces), iota((slots, traces), 0), own * 8 + rank)
    stores = []

    def place(start, width, rows):
        out_ref[:, start : start + width] = lax.dot_general(
            placing, rows, (((1,), (1,)), ((), ())), preferred_element_type=F32
        ).astype(BF16)
        store = pltpu.make_async_copy(
            out_ref.at[:, pl.ds(start, width)], out_hbm.at[:, pl.ds(start, width)], out_sems.at[len(stores)]
        )
        store.start()
        stores.append(store)

    which = iota((TAIL, traces), 0)
    row, col = bins_ref[...] // 18 + 1, bins_ref[...] % 18 + 1
    tail = jnp.where(which == 0, row, jnp.where(which == 1, col, 0)).astype(F32).astype(BF16)
    place(samples, TAIL, tail)

    wf = wf_ref[...].astype(F32)
    taps = [jnp.broadcast_to(column(wf[k : k + 1], 32), (32, 32)) for k in range(3)]
    lane = iota((32, 32), 1)
    for p in range(4):
        for u in range(6):
            block = jnp.zeros((32, 32), F32)
            for k in range(3):
                block = jnp.where(lane == 4 * u + p + k + 3, taps[k], block)
            w1[192 * p + 32 * u : 192 * p + 32 * (u + 1), :] = block.astype(BF16)
    wide = jnp.dot(
        ws_ref[...], picks((32, 256), iota((32, 256), 0), iota((32, 256), 1) % 32), preferred_element_type=F32
    ).astype(BF16)
    row = iota((192, 32), 0)
    channel = picks((192, 32), row % 64 // 8 * 4 + row % 4, iota((192, 32), 1))
    row = iota((192, 256), 0)
    apart = iota((192, 256), 1) // 32 - 2 * (row // 64) - row % 8 // 4
    total = jnp.zeros((192, 256), F32)
    for k in range(3):
        part = jnp.dot(channel, wide[32 * k : 32 * (k + 1)], preferred_element_type=F32)
        total = jnp.where(apart == k, part, total)
    w2[...] = total.astype(BF16)
    row = iota((64, 32), 0)
    of_row = jnp.where(row // 8 * 4 + row % 4 == iota((64, 32), 1), wn_ref[...].astype(F32), 0.0)
    wn[...] = jnp.broadcast_to(jnp.sum(of_row, axis=1, keepdims=True), wn.shape)

    loads[0].wait()
    xt[0:PAD, :] = jnp.zeros((PAD, traces), F32)
    xt[PAD + samples : rows, :] = jnp.zeros((rows - PAD - samples, traces), F32)
    for k in range(samples // 128):
        xt[PAD + 128 * k : PAD + 128 * (k + 1), :] = x_ref[:, 128 * k : 128 * (k + 1)].astype(F32).T

    def relu(value):
        return jnp.maximum(value.astype(BF16), jnp.zeros((), BF16))

    def hidden(j, h_ref, before):
        xs = xt[PAD + WIN * j : PAD + WIN * j + 32, :].astype(BF16)
        for p in range(4):
            h_ref[p, 0:64, :] = before[p, 192:256, :]
            h_ref[p, 64:256, :] = relu(
                jnp.dot(w1[192 * p : 192 * (p + 1), :], xs, preferred_element_type=F32)
            )

    sub = iota((3, 8, traces), 1)
    even = (sub & 1) == 0
    low = (sub & 2) == 0

    def pair(a, b, shift, mask):
        return jnp.where(mask, a + pltpu.roll(a, 8 - shift, 1), b + pltpu.roll(b, shift, 1))

    def second(j, h_ref):
        parts = []
        for p in range(4):
            o = jnp.dot(w2[...], h_ref[p], preferred_element_type=F32)
            o = jnp.maximum(o, 0.0).reshape(3, 64, traces) * wn[...][None]
            parts.append(jnp.sum(o.reshape(3, 8, 8, traces), axis=1))
        noise = pair(pair(parts[0], parts[1], 1, even), pair(parts[2], parts[3], 1, even), 2, low)
        x = xt[PAD + WIN * j : PAD + WIN * (j + 1), :]
        dt[WIN * j : WIN * (j + 1), :] = x - noise.reshape(WIN, traces)

    xs = xt[PAD - WIN : PAD - WIN + 32, :].astype(BF16)
    for p in range(4):
        hb[p, 192:224, :] = jnp.zeros((32, traces), BF16)
        hb[p, 224:256, :] = relu(
            jnp.dot(w1[192 * p + 160 : 192 * (p + 1), :], xs, preferred_element_type=F32)
        )
    hidden(0, ha, hb)
    for j in range(windows):
        this, other = hidden_bufs[j % 2], hidden_bufs[1 - j % 2]
        if j + 1 < windows:
            hidden(j + 1, other, this)
        else:
            inside = 32 * ((samples - WIN * j + 4) // 4)
            for p in range(4):
                this[p, inside:, :] = jnp.zeros((256 - inside, traces), BF16)
        second(j, this)
        while len(stores) - 1 < min(WIN * (j + 1), samples) // 256:
            start = 256 * (len(stores) - 1)
            place(start, 256, dt[start : start + 256, :].astype(BF16))
    for store in stores:
        store.wait()


def prepare_kernel(fold_ref, wv_ref, fold_out, w_out):
    bins = fold_out.shape[0]
    row = iota((bins, 16), 0)
    of_x = jnp.dot(
        picks((bins, 16), row // SIDE - 1, iota((bins, 16), 1)),
        fold_ref[...].astype(F32).astype(BF16),
        preferred_element_type=F32,
    )
    own = jnp.sum(jnp.where(row % SIDE - 1 == iota((bins, 16), 1), of_x, 0.0), axis=1, keepdims=True)
    fold_out[...] = jnp.broadcast_to(own, fold_out.shape)
    rows, cols = w_out.shape
    by_row = jnp.dot(
        picks((rows, 16), iota((rows, 16), 0) // 16 % 16, iota((rows, 16), 1)),
        wv_ref[...],
        preferred_element_type=F32,
    ).astype(BF16)
    row, col = iota((rows, cols), 0), iota((rows, cols), 1)
    dx = col // SIDE % 4 - row // 256
    dy = col % SIDE - row % 16
    near = (dx >= 0) & (dx < 3)
    dt = iota((27, cols), 1) // (4 * SIDE)
    total = jnp.zeros((rows, cols), F32)
    for k in range(9):
        taps = picks((27, cols), 3 * k + dt, iota((27, cols), 0))
        part = jnp.dot(by_row, taps, preferred_element_type=F32)
        total = jnp.where(near & (dx == k // 3) & (dy == k % 3), part, total)
    w_out[...] = total.astype(BF16)


def stack_kernel(recv_ref, fold_ref, main_ref, left_ref, right_ref):
    slots = recv_ref.shape[0]
    blocks, bins, _ = main_ref.shape
    samples = recv_ref.shape[1] - TAIL
    tail = recv_ref[:, samples:].astype(F32).T
    place = ((tail[0:1] - 1.0) * SIDE + (tail[1:2] - 1.0)).astype(jnp.int32)
    select = picks((bins, slots), iota((bins, slots), 0), place)
    for c in range(0, blocks - 1, 2):
        both = jnp.dot(select, recv_ref[:, 128 * c : 128 * (c + 2)], preferred_element_type=F32)
        main_ref[c] = both[:, :128]
        main_ref[c + 1] = both[:, 128:]
    main_ref[blocks - 1] = fold_ref[...]
    pad = jnp.zeros((24 - SIDE, 128), F32)
    at = lax.axis_index("xline")
    sides = ((left_ref, 0, at > 0), (right_ref, 16, at < lax.axis_size("xline") - 1))
    for c in range(blocks):
        lanes = slice(128 * c, 128 * (c + 1))
        for ref, first, wanted in sides:
            cols = [main_ref[c, pl.ds(first + k, SIDE, stride=SIDE), :] for k in range(2)]
            strip = jnp.concatenate([cols[0], pad, cols[1], pad], axis=0)
            ref[:, lanes] = jnp.where(wanted, strip, 0.0).astype(BF16)


def edges_kernel(main_ref, left_ref, right_ref, up_ref, down_ref, up, down):
    blocks, bins, _ = main_ref.shape
    for c in range(blocks):
        lanes = slice(128 * c, 128 * (c + 1))
        up[:, lanes] = main_ref[c, 0:STRIP, :]
        down[:, lanes] = main_ref[c, bins - STRIP : bins, :]
    for ref, first in ((left_ref, 0), (right_ref, 16)):
        strip = ref[...].astype(F32)
        for k in range(2):
            for r in range(2):
                at = r * SIDE + first + k
                up[at : at + 1, :] += strip[24 * k + r : 24 * k + r + 1, :]
                down[at : at + 1, :] += strip[24 * k + 16 + r : 24 * k + 17 + r, :]
    at = lax.axis_index("inline")
    wanted = (iota(up.shape, 0) < EDGE) & (at > 0)
    up_ref[...] = jnp.where(wanted, up[...], 0.0).astype(BF16)
    down_ref[...] = jnp.where(at < lax.axis_size("inline") - 1, down[...], 0.0).astype(BF16)


def add_sides(acc, left_ref, right_ref, start, count):
    for c in range(acc.shape[0]):
        lanes = slice(128 * c, 128 * (c + 1))
        for ref, first in ((left_ref, 0), (right_ref, 16)):
            strip = ref[:, lanes].astype(F32)
            for k in range(2):
                rows = pl.ds(start * SIDE + first + k, count, stride=SIDE)
                acc[c, rows, :] += strip[24 * k + start : 24 * k + start + count, :]


def make_taps(acc, vs, start, stop):
    blocks = acc.shape[0]
    samples = 128 * (blocks - 1)
    lane = iota((stop - start, samples), 1)
    fold = acc[blocks - 1, start:stop, :]
    inside = fold > 0.0
    fold = jnp.where(inside, fold, 1.0)
    v = jnp.concatenate([jnp.where(inside, acc[c, start:stop, :] / fold, 0.0) for c in range(blocks - 1)], axis=1)
    v = v.astype(BF16).astype(F32)
    vs[0, start:stop, :] = jnp.where(lane == 0, 0.0, pltpu.roll(v, 1, 1))
    vs[1, start:stop, :] = v
    vs[2, start:stop, :] = jnp.where(lane == samples - 1, 0.0, pltpu.roll(v, samples - 1, 1))


def convolve(m, vs, w_ref, block):
    taps = jnp.concatenate([vs[dt, EDGE * m : EDGE * (m + 2), :] for dt in range(3)], axis=0).astype(BF16)
    for c in range(0, vs.shape[2], 256):
        part = jnp.dot(w_ref[...], taps[:, c : c + 256], preferred_element_type=F32)
        block[:, :, :, c : c + 256] = part.astype(BF16).reshape(2, 16, 16, 256)


def inner_kernel(main_ref, left_ref, right_ref, w_ref, out_hbm, acc, vs, out, sems):
    acc[...] = main_ref[...]
    add_sides(acc, left_ref, right_ref, 2, 14)
    done, slots = EDGE // 8 * 8, out.shape[0]
    stores = []
    for m in range(1, 7):
        needed = EDGE * (m + 2) // 8 * 8 + 8 * (EDGE * (m + 2) % 8 > 0)
        make_taps(acc, vs, done, needed)
        done = needed
        k = m - 1
        if k >= slots:
            stores[k - slots].wait()
        convolve(m, vs, w_ref, out.at[k % slots])
        store = pltpu.make_async_copy(out.at[k % slots], out_hbm.at[pl.ds(2 * m, 2)], sems.at[k % slots])
        store.start()
        stores.append(store)
    for store in stores[6 - slots :]:
        store.wait()


def outer_kernel(main_ref, left_ref, right_ref, above_ref, below_ref, w_ref, _, out_hbm, acc, vs, out, sems):
    blocks, bins, _ = acc.shape
    top, bottom = 2 * EDGE, (bins - 2 * EDGE) // 8 * 8 - 8
    for c in range(blocks):
        lanes = slice(128 * c, 128 * (c + 1))
        acc[c, 0:top, :] = main_ref[c, 0:top, :]
        acc[c, bottom:bins, :] = main_ref[c, bottom:bins, :]
        acc[c, 0:STRIP, :] += above_ref[:, lanes].astype(F32)
        acc[c, bins - STRIP : bins, :] += below_ref[:, lanes].astype(F32)
    stores = []
    for k, (m, start, stop, row) in enumerate(((0, 0, top, 0), (7, bottom, bins, 14))):
        add_sides(acc, left_ref, right_ref, row, 4)
        make_taps(acc, vs, start, stop)
        convolve(m, vs, w_ref, out.at[k])
        store = pltpu.make_async_copy(out.at[k], out_hbm.at[pl.ds(2 * m, 2)], sems.at[k])
        store.start()
        stores.append(store)
    for store in stores:
        store.wait()


def neighbours(first, last, axis):
    size = lax.axis_size(axis)
    up = [(i, (i + 1) % size) for i in range(size)]
    down = [(j, i) for i, j in up]
    return lax.ppermute(last, axis, up), lax.ppermute(first, axis, down)


def body(traces, owner, bin_ids, fold, w_first, w_second, w_noise, w_volume):
    devices = lax.axis_size("inline") * lax.axis_size("xline")
    count, samples = traces.shape
    slots = devices * 8
    width = samples + TAIL
    vmem = pl.BlockSpec(memory_space=pltpu.VMEM)
    hbm = pl.BlockSpec(memory_space=pltpu.HBM)
    params = pltpu.CompilerParams(vmem_limit_bytes=24 << 20)
    rows = WIN * (-(-samples // WIN))
    outgoing = pl.pallas_call(
        denoise_kernel,
        out_shape=jax.ShapeDtypeStruct((slots, width), BF16),
        in_specs=[hbm] * 6,
        out_specs=hbm,
        scratch_shapes=[
            pltpu.VMEM((count, samples), BF16),
            pltpu.VMEM((1, count), jnp.int32),
            pltpu.VMEM((1, count), jnp.int32),
            pltpu.VMEM((3, 32), BF16),
            pltpu.VMEM((96, 32), BF16),
            pltpu.VMEM((1, 32), BF16),
            pltpu.VMEM((PAD + rows + 8, count), F32),
            pltpu.VMEM((rows, count), F32),
            pltpu.VMEM((4, 256, count), BF16),
            pltpu.VMEM((4, 256, count), BF16),
            pltpu.VMEM((768, 32), BF16),
            pltpu.VMEM((192, 256), BF16),
            pltpu.VMEM((64, count), F32),
            pltpu.VMEM((slots, width), BF16),
            pltpu.SemaphoreType.DMA((6,)),
            pltpu.SemaphoreType.DMA((samples // 256 + 1,)),
        ],
        compiler_params=pltpu.CompilerParams(vmem_limit_bytes=60 << 20),
        name="denoise",
    )(
        traces,
        owner.reshape(1, count),
        bin_ids.reshape(1, count),
        w_first.T,
        w_second.reshape(96, 32),
        w_noise.reshape(1, 32),
    )
    bins = BINS
    folds, w_taps = pl.pallas_call(
        prepare_kernel,
        out_shape=[jax.ShapeDtypeStruct((bins, TAIL), F32), jax.ShapeDtypeStruct((512, 12 * SIDE), BF16)],
        in_specs=[vmem] * 2,
        out_specs=[vmem] * 2,
        compiler_params=params,
        name="prepare",
    )(fold, w_volume)
    received = lax.all_to_all(
        outgoing.reshape(devices, 8, width), ("inline", "xline"), split_axis=0, concat_axis=0, tiled=True
    ).reshape(slots, width)
    strip = jax.ShapeDtypeStruct((48, width), BF16)
    edge = jax.ShapeDtypeStruct((STRIP, width), BF16)
    main, left, right = pl.pallas_call(
        stack_kernel,
        out_shape=[jax.ShapeDtypeStruct((width // 128, bins, 128), F32), strip, strip],
        in_specs=[vmem] * 2,
        out_specs=[vmem] * 3,
        compiler_params=params,
        name="stack",
    )(received, folds)
    from_left, from_right = neighbours(left, right, "xline")
    up, down = pl.pallas_call(
        edges_kernel,
        out_shape=[edge, edge],
        in_specs=[vmem] * 3,
        out_specs=[vmem] * 2,
        scratch_shapes=[pltpu.VMEM((STRIP, width), F32)] * 2,
        compiler_params=params,
        name="edges",
    )(main, from_left, from_right)
    above, below = neighbours(up, down, "inline")

    def scratch(slots):
        return [
            pltpu.VMEM((width // 128, bins, 128), F32),
            pltpu.VMEM((3, bins, samples), F32),
            pltpu.VMEM((slots, 2, 16, 16, samples), BF16),
            pltpu.SemaphoreType.DMA((slots,)),
        ]

    features = jax.ShapeDtypeStruct((16, 16, 16, samples), BF16)
    inner = pl.pallas_call(
        inner_kernel,
        out_shape=features,
        in_specs=[vmem] * 4,
        out_specs=hbm,
        scratch_shapes=scratch(3),
        compiler_params=params,
        cost_estimate=pl.CostEstimate(flops=1 << 32, transcendentals=0, bytes_accessed=8 << 20),
        name="inner",
    )(main, from_left, from_right, w_taps)
    return pl.pallas_call(
        outer_kernel,
        out_shape=features,
        in_specs=[vmem] * 6 + [hbm],
        out_specs=hbm,
        scratch_shapes=scratch(2),
        input_output_aliases={6: 0},
        compiler_params=params,
        name="outer",
    )(main, from_left, from_right, above, below, w_taps, inner)


def solution(mesh):
    placed = (
        P(("inline", "xline"), None),
        P(("inline", "xline"), None),
        P(("inline", "xline")),
        P("inline", "xline"),
        P(),
        P(),
        P(),
        P(),
    )
    return jax.shard_map(
        body,
        mesh=mesh,
        in_specs=placed,
        out_specs=P("inline", None, "xline", None),
        check_vma=False,
    )
```

```python
import jax
import jax.numpy as jnp
from jax import lax
from jax.experimental import pallas as pl
from jax.experimental.pallas import tpu as pltpu
from jax.sharding import PartitionSpec as P

F32 = jnp.float32
BF16 = jnp.bfloat16
WIN = 24
PAD = 24
SIDE = 18
BINS = 328
EDGE = 2 * SIDE
STRIP = 40
TAIL = 128


def iota(shape, dim):
    return lax.broadcasted_iota(jnp.int32, shape, dim)


def picks(shape, row, col):
    return jnp.where(jnp.broadcast_to(row == col, shape), 1.0, 0.0).astype(BF16)


def column(vector, size):
    eye = iota((size, size), 0) == iota((size, size), 1)
    return jnp.sum(jnp.where(eye, vector, 0.0), axis=1, keepdims=True)


def denoise_kernel(*refs):
    ins, out_hbm, bufs = refs[:6], refs[6], refs[7:13]
    xt, dt, ha, hb, w1, w2, wn, out_ref, in_sems, out_sems = refs[13:]
    x_ref, own_ref, bins_ref, wf_ref, ws_ref, wn_ref = bufs
    loads = [pltpu.make_async_copy(src, dst, in_sems.at[k]) for k, (src, dst) in enumerate(zip(ins, bufs))]
    for load in loads:
        load.start()
    traces, samples = x_ref.shape
    slots = out_ref.shape[0]
    rows = xt.shape[0]
    windows = -(-samples // WIN)
    hidden_bufs = (ha, hb)

    for load in loads:
        load.wait()

    own = own_ref[...]
    own_col = column(own.astype(F32), traces).astype(jnp.int32)
    earlier = (own_col == own) & (iota((traces, traces), 0) < iota((traces, traces), 1))
    rank = jnp.sum(jnp.where(earlier, 1.0, 0.0), axis=0, keepdims=True).astype(jnp.int32)
    placing = picks((slots, traces), iota((slots, traces), 0), own * 8 + rank)
    stores = []

    def place(start, width, rows):
        out_ref[:, start : start + width] = lax.dot_general(
            placing, rows, (((1,), (1,)), ((), ())), preferred_element_type=F32
        ).astype(BF16)
        store = pltpu.make_async_copy(
            out_ref.at[:, pl.ds(start, width)], out_hbm.at[:, pl.ds(start, width)], out_sems.at[len(stores)]
        )
        store.start()
        stores.append(store)

    wf = wf_ref[...].astype(F32)
    taps = [jnp.broadcast_to(column(wf[k : k + 1], 32), (32, 32)) for k in range(3)]
    lane = iota((32, 32), 1)
    for p in range(4):
        for u in range(6):
            block = jnp.zeros((32, 32), F32)
            for k in range(3):
                block = jnp.where(lane == 4 * u + p + k + 3, taps[k], block)
            w1[192 * p + 32 * u : 192 * p + 32 * (u + 1), :] = block.astype(BF16)
    wide = jnp.dot(
        ws_ref[...], picks((32, 256), iota((32, 256), 0), iota((32, 256), 1) % 32), preferred_element_type=F32
    ).astype(BF16)
    row = iota((192, 32), 0)
    channel = picks((192, 32), row % 64 // 8 * 4 + row % 4, iota((192, 32), 1))
    row = iota((192, 256), 0)
    apart = iota((192, 256), 1) // 32 - 2 * (row // 64) - row % 8 // 4
    total = jnp.zeros((192, 256), F32)
    for k in range(3):
        part = jnp.dot(channel, wide[32 * k : 32 * (k + 1)], preferred_element_type=F32)
        total = jnp.where(apart == k, part, total)
    w2[...] = total.astype(BF16)
    row = iota((64, 32), 0)
    of_row = jnp.where(row // 8 * 4 + row % 4 == iota((64, 32), 1), wn_ref[...].astype(F32), 0.0)
    wn[...] = jnp.broadcast_to(jnp.sum(of_row, axis=1, keepdims=True), wn.shape)

    xt[0:PAD, :] = jnp.zeros((PAD, traces), F32)
    xt[PAD + samples : rows, :] = jnp.zeros((rows - PAD - samples, traces), F32)
    for k in range(samples // 128):
        xt[PAD + 128 * k : PAD + 128 * (k + 1), :] = x_ref[:, 128 * k : 128 * (k + 1)].astype(F32).T

    def relu(value):
        return jnp.maximum(value.astype(BF16), jnp.zeros((), BF16))

    def hidden(j, h_ref, before):
        xs = xt[PAD + WIN * j : PAD + WIN * j + 32, :].astype(BF16)
        for p in range(4):
            h_ref[p, 0:64, :] = before[p, 192:256, :]
            h_ref[p, 64:256, :] = relu(
                jnp.dot(w1[192 * p : 192 * (p + 1), :], xs, preferred_element_type=F32)
            )

    sub = iota((3, 8, traces), 1)
    even = (sub & 1) == 0
    low = (sub & 2) == 0

    def pair(a, b, shift, mask):
        return jnp.where(mask, a + pltpu.roll(a, 8 - shift, 1), b + pltpu.roll(b, shift, 1))

    def second(j, h_ref):
        parts = []
        for p in range(4):
            o = jnp.dot(w2[...], h_ref[p], preferred_element_type=F32)
            o = jnp.maximum(o, 0.0).reshape(3, 64, traces) * wn[...][None]
            parts.append(jnp.sum(o.reshape(3, 8, 8, traces), axis=1))
        noise = pair(pair(parts[0], parts[1], 1, even), pair(parts[2], parts[3], 1, even), 2, low)
        x = xt[PAD + WIN * j : PAD + WIN * (j + 1), :]
        dt[WIN * j : WIN * (j + 1), :] = x - noise.reshape(WIN, traces)

    xs = xt[PAD - WIN : PAD - WIN + 32, :].astype(BF16)
    for p in range(4):
        hb[p, 192:224, :] = jnp.zeros((32, traces), BF16)
        hb[p, 224:256, :] = relu(
            jnp.dot(w1[192 * p + 160 : 192 * (p + 1), :], xs, preferred_element_type=F32)
        )
    hidden(0, ha, hb)
    placed = 0
    which = iota((TAIL, traces), 0)
    row, col = bins_ref[...] // 18 + 1, bins_ref[...] % 18 + 1
    tail = jnp.where(which == 0, row, jnp.where(which == 1, col, 0)).astype(F32).astype(BF16)
    place(samples, TAIL, tail)
    for j in range(windows):
        this, other = hidden_bufs[j % 2], hidden_bufs[1 - j % 2]
        if j + 1 < windows:
            hidden(j + 1, other, this)
        else:
            inside = 32 * ((samples - WIN * j + 4) // 4)
            for p in range(4):
                this[p, inside:, :] = jnp.zeros((256 - inside, traces), BF16)
        second(j, this)
        ready = min(WIN * (j + 1), samples)
        while placed < samples and placed + 256 <= ready:
            place(placed, 256, dt[placed : placed + 256, :].astype(BF16))
            placed += 256
    for store in stores:
        store.wait()


def prepare_kernel(fold_ref, wv_ref, fold_out, w_out):
    bins = fold_out.shape[0]
    row = iota((bins, 16), 0)
    of_x = jnp.dot(
        picks((bins, 16), row // SIDE - 1, iota((bins, 16), 1)),
        fold_ref[...].astype(F32).astype(BF16),
        preferred_element_type=F32,
    )
    own = jnp.sum(jnp.where(row % SIDE - 1 == iota((bins, 16), 1), of_x, 0.0), axis=1, keepdims=True)
    fold_out[...] = jnp.broadcast_to(own, fold_out.shape)
    rows, cols = w_out.shape
    by_row = jnp.dot(
        picks((rows, 16), iota((rows, 16), 0) // 16 % 16, iota((rows, 16), 1)),
        wv_ref[...],
        preferred_element_type=F32,
    ).astype(BF16)
    row, col = iota((rows, cols), 0), iota((rows, cols), 1)
    dx = col // SIDE % 4 - row // 256
    dy = col % SIDE - row % 16
    near = (dx >= 0) & (dx < 3)
    dt = iota((27, cols), 1) // (4 * SIDE)
    total = jnp.zeros((rows, cols), F32)
    for k in range(9):
        taps = picks((27, cols), 3 * k + dt, iota((27, cols), 0))
        part = jnp.dot(by_row, taps, preferred_element_type=F32)
        total = jnp.where(near & (dx == k // 3) & (dy == k % 3), part, total)
    w_out[...] = total.astype(BF16)


def stack_kernel(recv_ref, fold_ref, main_ref, left_ref, right_ref):
    slots = recv_ref.shape[0]
    blocks, bins, _ = main_ref.shape
    samples = recv_ref.shape[1] - TAIL
    tail = recv_ref[:, samples:].astype(F32).T
    place = ((tail[0:1] - 1.0) * SIDE + (tail[1:2] - 1.0)).astype(jnp.int32)
    select = picks((bins, slots), iota((bins, slots), 0), place)
    for c in range(0, blocks - 1, 2):
        both = jnp.dot(select, recv_ref[:, 128 * c : 128 * (c + 2)], preferred_element_type=F32)
        main_ref[c] = both[:, :128]
        main_ref[c + 1] = both[:, 128:]
    main_ref[blocks - 1] = fold_ref[...]
    pad = jnp.zeros((STRIP - EDGE, 128), F32)
    at = lax.axis_index("xline")
    sides = ((left_ref, 0, at > 0), (right_ref, 16, at < lax.axis_size("xline") - 1))
    for c in range(blocks):
        lanes = slice(128 * c, 128 * (c + 1))
        for ref, first, wanted in sides:
            cols = [main_ref[c, pl.ds(first + k, SIDE, stride=SIDE), :] for k in range(2)]
            strip = jnp.concatenate([cols[0], cols[1], pad], axis=0)
            ref[:, lanes] = jnp.where(wanted, strip, 0.0).astype(BF16)


def edges_kernel(main_ref, left_ref, right_ref, up_ref, down_ref, up, down):
    blocks, bins, _ = main_ref.shape
    for c in range(blocks):
        lanes = slice(128 * c, 128 * (c + 1))
        up[:, lanes] = main_ref[c, 0:STRIP, :]
        down[:, lanes] = main_ref[c, bins - STRIP : bins, :]
    for ref, first in ((left_ref, 0), (right_ref, 16)):
        strip = ref[...].astype(F32)
        for k in range(2):
            for r in range(2):
                at = r * SIDE + first + k
                up[at : at + 1, :] += strip[SIDE * k + r : SIDE * k + r + 1, :]
                down[at : at + 1, :] += strip[SIDE * k + 16 + r : SIDE * k + 17 + r, :]
    at = lax.axis_index("inline")
    wanted = (iota(up.shape, 0) < EDGE) & (at > 0)
    up_ref[...] = jnp.where(wanted, up[...], 0.0).astype(BF16)
    down_ref[...] = jnp.where(at < lax.axis_size("inline") - 1, down[...], 0.0).astype(BF16)


def add_sides(acc, left_ref, right_ref, start, count):
    for c in range(acc.shape[0]):
        lanes = slice(128 * c, 128 * (c + 1))
        for ref, first in ((left_ref, 0), (right_ref, 16)):
            strip = ref[:, lanes].astype(F32)
            for k in range(2):
                rows = pl.ds(start * SIDE + first + k, count, stride=SIDE)
                acc[c, rows, :] += strip[SIDE * k + start : SIDE * k + start + count, :]


def make_taps(acc, vs, start, stop):
    blocks = acc.shape[0]
    samples = 128 * (blocks - 1)
    lane = iota((stop - start, samples), 1)
    fold = acc[blocks - 1, start:stop, :]
    inside = fold > 0.0
    fold = jnp.where(inside, fold, 1.0)
    v = jnp.concatenate([jnp.where(inside, acc[c, start:stop, :] / fold, 0.0) for c in range(blocks - 1)], axis=1)
    v = v.astype(BF16).astype(F32)
    vs[0, start:stop, :] = jnp.where(lane == 0, 0.0, pltpu.roll(v, 1, 1))
    vs[1, start:stop, :] = v
    vs[2, start:stop, :] = jnp.where(lane == samples - 1, 0.0, pltpu.roll(v, samples - 1, 1))


def convolve(m, vs, w_ref, block):
    taps = jnp.concatenate([vs[dt, EDGE * m : EDGE * (m + 2), :] for dt in range(3)], axis=0).astype(BF16)
    for c in range(0, vs.shape[2], 256):
        part = jnp.dot(w_ref[...], taps[:, c : c + 256], preferred_element_type=F32)
        block[:, :, :, c : c + 256] = part.astype(BF16).reshape(2, 16, 16, 256)


def inner_kernel(main_ref, left_ref, right_ref, w_ref, out_hbm, acc, vs, out, sems):
    acc[...] = main_ref[...]
    add_sides(acc, left_ref, right_ref, 2, 14)
    slots = out.shape[0]
    stores = []
    ends = [EDGE // 8 * 8] + [-(-EDGE * (m + 2) // 8) * 8 for m in range(1, 7)]
    make_taps(acc, vs, ends[0], ends[1])
    for k in range(6):
        if k >= slots:
            stores[k - slots].wait()
        if k < 5:
            make_taps(acc, vs, ends[k + 1], ends[k + 2])
        convolve(k + 1, vs, w_ref, out.at[k % slots])
        store = pltpu.make_async_copy(out.at[k % slots], out_hbm.at[pl.ds(2 * k + 2, 2)], sems.at[k % slots])
        store.start()
        stores.append(store)
    for store in stores[6 - slots :]:
        store.wait()


def outer_kernel(main_ref, left_ref, right_ref, above_ref, below_ref, w_ref, _, out_hbm, acc, vs, out, sems):
    blocks, bins, _ = acc.shape
    top, bottom = 2 * EDGE, (bins - 2 * EDGE) // 8 * 8 - 8
    for c in range(blocks):
        lanes = slice(128 * c, 128 * (c + 1))
        acc[c, 0:top, :] = main_ref[c, 0:top, :]
        acc[c, bottom:bins, :] = main_ref[c, bottom:bins, :]
        acc[c, 0:STRIP, :] += above_ref[:, lanes].astype(F32)
        acc[c, bins - STRIP : bins, :] += below_ref[:, lanes].astype(F32)
    stores = []
    for k, (m, start, stop, row) in enumerate(((0, 0, top, 0), (7, bottom, bins, 14))):
        add_sides(acc, left_ref, right_ref, row, 4)
        make_taps(acc, vs, start, stop)
        convolve(m, vs, w_ref, out.at[k])
        store = pltpu.make_async_copy(out.at[k], out_hbm.at[pl.ds(2 * m, 2)], sems.at[k])
        store.start()
        stores.append(store)
    for store in stores:
        store.wait()


def neighbours(first, last, axis):
    size = lax.axis_size(axis)
    up = [(i, (i + 1) % size) for i in range(size)]
    down = [(j, i) for i, j in up]
    return lax.ppermute(last, axis, up), lax.ppermute(first, axis, down)


def body(traces, owner, bin_ids, fold, w_first, w_second, w_noise, w_volume):
    devices = lax.axis_size("inline") * lax.axis_size("xline")
    count, samples = traces.shape
    slots = devices * 8
    width = samples + TAIL
    vmem = pl.BlockSpec(memory_space=pltpu.VMEM)
    hbm = pl.BlockSpec(memory_space=pltpu.HBM)
    params = pltpu.CompilerParams(vmem_limit_bytes=24 << 20)
    rows = WIN * (-(-samples // WIN))
    outgoing = pl.pallas_call(
        denoise_kernel,
        out_shape=jax.ShapeDtypeStruct((slots, width), BF16),
        in_specs=[hbm] * 6,
        out_specs=hbm,
        scratch_shapes=[
            pltpu.VMEM((count, samples), BF16),
            pltpu.VMEM((1, count), jnp.int32),
            pltpu.VMEM((1, count), jnp.int32),
            pltpu.VMEM((3, 32), BF16),
            pltpu.VMEM((96, 32), BF16),
            pltpu.VMEM((1, 32), BF16),
            pltpu.VMEM((PAD + rows + 8, count), F32),
            pltpu.VMEM((rows, count), F32),
            pltpu.VMEM((4, 256, count), BF16),
            pltpu.VMEM((4, 256, count), BF16),
            pltpu.VMEM((768, 32), BF16),
            pltpu.VMEM((192, 256), BF16),
            pltpu.VMEM((64, count), F32),
            pltpu.VMEM((slots, width), BF16),
            pltpu.SemaphoreType.DMA((6,)),
            pltpu.SemaphoreType.DMA((samples // 256 + 1,)),
        ],
        compiler_params=pltpu.CompilerParams(vmem_limit_bytes=60 << 20),
        name="denoise",
    )(
        traces,
        owner.reshape(1, count),
        bin_ids.reshape(1, count),
        w_first.T,
        w_second.reshape(96, 32),
        w_noise.reshape(1, 32),
    )
    bins = BINS
    folds, w_taps = pl.pallas_call(
        prepare_kernel,
        out_shape=[jax.ShapeDtypeStruct((bins, TAIL), F32), jax.ShapeDtypeStruct((512, 12 * SIDE), BF16)],
        in_specs=[vmem] * 2,
        out_specs=[vmem] * 2,
        compiler_params=params,
        name="prepare",
    )(fold, w_volume)
    received = lax.all_to_all(
        outgoing.reshape(devices, 8, width), ("inline", "xline"), split_axis=0, concat_axis=0, tiled=True
    ).reshape(slots, width)
    edge = jax.ShapeDtypeStruct((STRIP, width), BF16)
    main, left, right = pl.pallas_call(
        stack_kernel,
        out_shape=[jax.ShapeDtypeStruct((width // 128, bins, 128), F32), edge, edge],
        in_specs=[vmem] * 2,
        out_specs=[vmem] * 3,
        compiler_params=params,
        name="stack",
    )(received, folds)
    from_left, from_right = neighbours(left, right, "xline")
    up, down = pl.pallas_call(
        edges_kernel,
        out_shape=[edge, edge],
        in_specs=[vmem] * 3,
        out_specs=[vmem] * 2,
        scratch_shapes=[pltpu.VMEM((STRIP, width), F32)] * 2,
        compiler_params=params,
        name="edges",
    )(main, from_left, from_right)
    above, below = neighbours(up, down, "inline")

    def scratch(slots):
        return [
            pltpu.VMEM((width // 128, bins, 128), F32),
            pltpu.VMEM((3, bins, samples), F32),
            pltpu.VMEM((slots, 2, 16, 16, samples), BF16),
            pltpu.SemaphoreType.DMA((slots,)),
        ]

    features = jax.ShapeDtypeStruct((16, 16, 16, samples), BF16)
    inner = pl.pallas_call(
        inner_kernel,
        out_shape=features,
        in_specs=[vmem] * 4,
        out_specs=hbm,
        scratch_shapes=scratch(3),
        compiler_params=params,
        cost_estimate=pl.CostEstimate(flops=1 << 32, transcendentals=0, bytes_accessed=8 << 20),
        name="inner",
    )(main, from_left, from_right, w_taps)
    return pl.pallas_call(
        outer_kernel,
        out_shape=features,
        in_specs=[vmem] * 6 + [hbm],
        out_specs=hbm,
        scratch_shapes=scratch(2),
        input_output_aliases={6: 0},
        compiler_params=params,
        name="outer",
    )(main, from_left, from_right, above, below, w_taps, inner)


def solution(mesh):
    placed = (
        P(("inline", "xline"), None),
        P(("inline", "xline"), None),
        P(("inline", "xline")),
        P("inline", "xline"),
        P(),
        P(),
        P(),
        P(),
    )
    return jax.shard_map(
        body,
        mesh=mesh,
        in_specs=placed,
        out_specs=P("inline", None, "xline", None),
        check_vma=False,
    )
```

```python
import jax
import jax.numpy as jnp
from jax import lax
from jax.experimental import pallas as pl
from jax.experimental.pallas import tpu as pltpu
from jax.sharding import PartitionSpec as P

F32 = jnp.float32
BF16 = jnp.bfloat16
WIN = 24
PAD = 24
SIDE = 18
BINS = 328
EDGE = 2 * SIDE
STRIP = 40
TAIL = 128


def iota(shape, dim):
    return lax.broadcasted_iota(jnp.int32, shape, dim)


def picks(shape, row, col):
    return jnp.where(jnp.broadcast_to(row == col, shape), 1.0, 0.0).astype(BF16)


def column(vector, size):
    eye = iota((size, size), 0) == iota((size, size), 1)
    return jnp.sum(jnp.where(eye, vector, 0.0), axis=1, keepdims=True)


def denoise_kernel(*refs):
    ins, out_hbm, bufs = refs[:6], refs[6], refs[7:13]
    xt, dt, ha, hb, w1, w2, wn, out_ref, in_sems, out_sems = refs[13:]
    x_ref, own_ref, bins_ref, wf_ref, ws_ref, wn_ref = bufs
    loads = [pltpu.make_async_copy(src, dst, in_sems.at[k]) for k, (src, dst) in enumerate(zip(ins, bufs))]
    for load in loads:
        load.start()
    traces, samples = x_ref.shape
    slots = out_ref.shape[0]
    rows = xt.shape[0]
    windows = -(-samples // WIN)
    hidden_bufs = (ha, hb)

    for load in loads:
        load.wait()

    own = own_ref[...]
    own_col = column(own.astype(F32), traces).astype(jnp.int32)
    earlier = (own_col == own) & (iota((traces, traces), 0) < iota((traces, traces), 1))
    rank = jnp.sum(jnp.where(earlier, 1.0, 0.0), axis=0, keepdims=True).astype(jnp.int32)
    placing = picks((slots, traces), iota((slots, traces), 0), own * 8 + rank)
    stores = []

    def place(start, width, rows):
        out_ref[:, start : start + width] = lax.dot_general(
            placing, rows, (((1,), (1,)), ((), ())), preferred_element_type=F32
        ).astype(BF16)
        store = pltpu.make_async_copy(
            out_ref.at[:, pl.ds(start, width)], out_hbm.at[:, pl.ds(start, width)], out_sems.at[len(stores)]
        )
        store.start()
        stores.append(store)

    wf = wf_ref[...].astype(F32)
    taps = [jnp.broadcast_to(column(wf[k : k + 1], 32), (32, 32)) for k in range(3)]
    lane = iota((32, 32), 1)
    for p in range(4):
        for u in range(6):
            block = jnp.zeros((32, 32), F32)
            for k in range(3):
                block = jnp.where(lane == 4 * u + p + k + 3, taps[k], block)
            w1[192 * p + 32 * u : 192 * p + 32 * (u + 1), :] = block.astype(BF16)
    wide = jnp.dot(
        ws_ref[...], picks((32, 256), iota((32, 256), 0), iota((32, 256), 1) % 32), preferred_element_type=F32
    ).astype(BF16)
    row = iota((192, 32), 0)
    channel = picks((192, 32), row % 64 // 8 * 4 + row % 4, iota((192, 32), 1))
    row = iota((192, 256), 0)
    apart = iota((192, 256), 1) // 32 - 2 * (row // 64) - row % 8 // 4
    total = jnp.zeros((192, 256), F32)
    for k in range(3):
        part = jnp.dot(channel, wide[32 * k : 32 * (k + 1)], preferred_element_type=F32)
        total = jnp.where(apart == k, part, total)
    w2[...] = total.astype(BF16)
    row = iota((64, 32), 0)
    of_row = jnp.where(row // 8 * 4 + row % 4 == iota((64, 32), 1), wn_ref[...].astype(F32), 0.0)
    wn[...] = jnp.broadcast_to(jnp.sum(of_row, axis=1, keepdims=True), wn.shape)

    xt[0:PAD, :] = jnp.zeros((PAD, traces), F32)
    xt[PAD + samples : rows, :] = jnp.zeros((rows - PAD - samples, traces), F32)
    for k in range(samples // 128):
        xt[PAD + 128 * k : PAD + 128 * (k + 1), :] = x_ref[:, 128 * k : 128 * (k + 1)].astype(F32).T

    def relu(value):
        return jnp.maximum(value.astype(BF16), jnp.zeros((), BF16))

    def hidden(j, h_ref, before):
        xs = xt[PAD + WIN * j : PAD + WIN * j + 32, :].astype(BF16)
        for p in range(4):
            h_ref[p, 0:64, :] = before[p, 192:256, :]
            h_ref[p, 64:256, :] = relu(
                jnp.dot(w1[192 * p : 192 * (p + 1), :], xs, preferred_element_type=F32)
            )

    sub = iota((3, 8, traces), 1)
    even = (sub & 1) == 0
    low = (sub & 2) == 0

    def pair(a, b, shift, mask):
        return jnp.where(mask, a + pltpu.roll(a, 8 - shift, 1), b + pltpu.roll(b, shift, 1))

    def second(j, h_ref):
        parts = []
        for p in range(4):
            o = jnp.dot(w2[...], h_ref[p], preferred_element_type=F32)
            o = jnp.maximum(o, 0.0).reshape(3, 64, traces) * wn[...][None]
            parts.append(jnp.sum(o.reshape(3, 8, 8, traces), axis=1))
        noise = pair(pair(parts[0], parts[1], 1, even), pair(parts[2], parts[3], 1, even), 2, low)
        x = xt[PAD + WIN * j : PAD + WIN * (j + 1), :]
        dt[WIN * j : WIN * (j + 1), :] = x - noise.reshape(WIN, traces)

    xs = xt[PAD - WIN : PAD - WIN + 32, :].astype(BF16)
    for p in range(4):
        hb[p, 192:224, :] = jnp.zeros((32, traces), BF16)
        hb[p, 224:256, :] = relu(
            jnp.dot(w1[192 * p + 160 : 192 * (p + 1), :], xs, preferred_element_type=F32)
        )
    hidden(0, ha, hb)
    placed = 0
    which = iota((TAIL, traces), 0)
    row, col = bins_ref[...] // 18 + 1, bins_ref[...] % 18 + 1
    tail = jnp.where(which == 0, row, jnp.where(which == 1, col, 0)).astype(F32).astype(BF16)
    place(samples, TAIL, tail)
    for j in range(windows):
        this, other = hidden_bufs[j % 2], hidden_bufs[1 - j % 2]
        if j + 1 < windows:
            hidden(j + 1, other, this)
        else:
            inside = 32 * ((samples - WIN * j + 4) // 4)
            for p in range(4):
                this[p, inside:, :] = jnp.zeros((256 - inside, traces), BF16)
        second(j, this)
        ready = min(WIN * (j + 1), samples)
        while placed < samples and placed + 256 <= ready:
            place(placed, 256, dt[placed : placed + 256, :].astype(BF16))
            placed += 256
    for store in stores:
        store.wait()


def prepare_kernel(fold_ref, wv_ref, fold_out, w_out):
    bins = fold_out.shape[0]
    row = iota((bins, 16), 0)
    of_x = jnp.dot(
        picks((bins, 16), row // SIDE - 1, iota((bins, 16), 1)),
        fold_ref[...].astype(F32).astype(BF16),
        preferred_element_type=F32,
    )
    own = jnp.sum(jnp.where(row % SIDE - 1 == iota((bins, 16), 1), of_x, 0.0), axis=1, keepdims=True)
    fold_out[...] = jnp.broadcast_to(own, fold_out.shape)
    rows, cols = w_out.shape
    by_row = jnp.dot(
        picks((rows, 16), iota((rows, 16), 0) // 16 % 16, iota((rows, 16), 1)),
        wv_ref[...],
        preferred_element_type=F32,
    ).astype(BF16)
    row, col = iota((rows, cols), 0), iota((rows, cols), 1)
    dx = col // SIDE % 4 - row // 256
    dy = col % SIDE - row % 16
    near = (dx >= 0) & (dx < 3)
    dt = iota((27, cols), 1) // (4 * SIDE)
    total = jnp.zeros((rows, cols), F32)
    for k in range(9):
        taps = picks((27, cols), 3 * k + dt, iota((27, cols), 0))
        part = jnp.dot(by_row, taps, preferred_element_type=F32)
        total = jnp.where(near & (dx == k // 3) & (dy == k % 3), part, total)
    w_out[...] = total.astype(BF16)


def bins_of(recv_ref):
    tail = recv_ref[:, recv_ref.shape[1] - TAIL :].astype(F32).T
    return ((tail[0:1] - 1.0) * SIDE + (tail[1:2] - 1.0)).astype(jnp.int32)


def sides_kernel(recv_ref, fold_ref, left_ref, right_ref):
    slots, width = recv_ref.shape
    row = iota((2 * STRIP, slots), 0)
    at = row % STRIP
    wanted_bin = at % SIDE * SIDE + at // SIDE + row // STRIP * 16
    wanted_bin = jnp.where(at < EDGE, wanted_bin, -1000)
    select = picks((2 * STRIP, slots), wanted_bin, bins_of(recv_ref))
    at = lax.axis_index("xline")
    sides = ((left_ref, 0, at > 0), (right_ref, 16, at < lax.axis_size("xline") - 1))
    for c in range(0, width - TAIL, 256):
        part = jnp.dot(select, recv_ref[:, c : c + 256], preferred_element_type=F32)
        for k, (ref, _, wanted) in enumerate(sides):
            ref[:, c : c + 256] = jnp.where(wanted, part[STRIP * k : STRIP * (k + 1)], 0.0).astype(BF16)
    pad = jnp.zeros((STRIP - EDGE, TAIL), F32)
    for ref, first, wanted in sides:
        cols = [fold_ref[pl.ds(first + k, SIDE, stride=SIDE), :] for k in range(2)]
        strip = jnp.concatenate([cols[0], cols[1], pad], axis=0)
        ref[:, width - TAIL :] = jnp.where(wanted, strip, 0.0).astype(BF16)


def stack_kernel(recv_ref, fold_ref, main_ref):
    slots = recv_ref.shape[0]
    blocks, bins, _ = main_ref.shape
    select = picks((bins, slots), iota((bins, slots), 0), bins_of(recv_ref))
    for c in range(0, blocks - 1, 2):
        both = jnp.dot(select, recv_ref[:, 128 * c : 128 * (c + 2)], preferred_element_type=F32)
        main_ref[c] = both[:, :128]
        main_ref[c + 1] = both[:, 128:]
    main_ref[blocks - 1] = fold_ref[...]


def edges_kernel(main_ref, left_ref, right_ref, up_ref, down_ref, up, down):
    blocks, bins, _ = main_ref.shape
    for c in range(blocks):
        lanes = slice(128 * c, 128 * (c + 1))
        up[:, lanes] = main_ref[c, 0:STRIP, :]
        down[:, lanes] = main_ref[c, bins - STRIP : bins, :]
    for ref, first in ((left_ref, 0), (right_ref, 16)):
        strip = ref[...].astype(F32)
        for k in range(2):
            for r in range(2):
                at = r * SIDE + first + k
                up[at : at + 1, :] += strip[SIDE * k + r : SIDE * k + r + 1, :]
                down[at : at + 1, :] += strip[SIDE * k + 16 + r : SIDE * k + 17 + r, :]
    at = lax.axis_index("inline")
    wanted = (iota(up.shape, 0) < EDGE) & (at > 0)
    up_ref[...] = jnp.where(wanted, up[...], 0.0).astype(BF16)
    down_ref[...] = jnp.where(at < lax.axis_size("inline") - 1, down[...], 0.0).astype(BF16)


def add_sides(acc, left_ref, right_ref, start, count):
    for c in range(acc.shape[0]):
        lanes = slice(128 * c, 128 * (c + 1))
        for ref, first in ((left_ref, 0), (right_ref, 16)):
            strip = ref[:, lanes].astype(F32)
            for k in range(2):
                rows = pl.ds(start * SIDE + first + k, count, stride=SIDE)
                acc[c, rows, :] += strip[SIDE * k + start : SIDE * k + start + count, :]


def make_taps(acc, vs, start, stop):
    blocks = acc.shape[0]
    samples = 128 * (blocks - 1)
    lane = iota((stop - start, samples), 1)
    fold = acc[blocks - 1, start:stop, :]
    inside = fold > 0.0
    fold = jnp.where(inside, fold, 1.0)
    v = jnp.concatenate([jnp.where(inside, acc[c, start:stop, :] / fold, 0.0) for c in range(blocks - 1)], axis=1)
    v = v.astype(BF16).astype(F32)
    vs[0, start:stop, :] = jnp.where(lane == 0, 0.0, pltpu.roll(v, 1, 1))
    vs[1, start:stop, :] = v
    vs[2, start:stop, :] = jnp.where(lane == samples - 1, 0.0, pltpu.roll(v, samples - 1, 1))


def convolve(m, vs, w_ref, block, out_hbm, sem, width):
    taps = jnp.concatenate([vs[dt, EDGE * m : EDGE * (m + 2), :] for dt in range(3)], axis=0).astype(BF16)
    stores = []
    for c in range(0, vs.shape[2], 256):
        part = jnp.dot(w_ref[...], taps[:, c : c + 256], preferred_element_type=F32)
        block[:, :, :, c : c + 256] = part.astype(BF16).reshape(2, 16, 16, 256)
        if (c + 256) % width == 0:
            lanes = pl.ds(c + 256 - width, width)
            store = pltpu.make_async_copy(
                block.at[:, :, :, lanes], out_hbm.at[pl.ds(2 * m, 2), :, :, lanes], sem.at[len(stores)]
            )
            store.start()
            stores.append(store)
    return stores


def inner_kernel(main_ref, left_ref, right_ref, w_ref, out_hbm, acc, vs, out, sems):
    acc[...] = main_ref[...]
    add_sides(acc, left_ref, right_ref, 2, 14)
    stores = []
    ends = [EDGE // 8 * 8] + [-(-EDGE * (m + 2) // 8) * 8 for m in range(1, 7)]
    make_taps(acc, vs, ends[0], ends[1])
    for k in range(6):
        if k < 5:
            make_taps(acc, vs, ends[k + 1], ends[k + 2])
        stores += convolve(k + 1, vs, w_ref, out.at[k], out_hbm, sems.at[k], 1024 if k < 5 else 512)
    for store in stores:
        store.wait()


def outer_kernel(main_ref, left_ref, right_ref, above_ref, below_ref, w_ref, _, out_hbm, acc, vs, out, sems):
    blocks, bins, _ = acc.shape
    top, bottom = 2 * EDGE, (bins - 2 * EDGE) // 8 * 8 - 8
    for c in range(blocks):
        lanes = slice(128 * c, 128 * (c + 1))
        acc[c, 0:top, :] = main_ref[c, 0:top, :]
        acc[c, bottom:bins, :] = main_ref[c, bottom:bins, :]
        acc[c, 0:STRIP, :] += above_ref[:, lanes].astype(F32)
        acc[c, bins - STRIP : bins, :] += below_ref[:, lanes].astype(F32)
    for start, stop, row in ((0, top, 0), (bottom, bins, 14)):
        add_sides(acc, left_ref, right_ref, row, 4)
        make_taps(acc, vs, start, stop)
    stores = convolve(0, vs, w_ref, out.at[0], out_hbm, sems.at[0], 512)
    stores += convolve(7, vs, w_ref, out.at[1], out_hbm, sems.at[1], 512)
    for store in stores:
        store.wait()


def neighbours(first, last, axis):
    size = lax.axis_size(axis)
    up = [(i, (i + 1) % size) for i in range(size)]
    down = [(j, i) for i, j in up]
    return lax.ppermute(last, axis, up), lax.ppermute(first, axis, down)


def body(traces, owner, bin_ids, fold, w_first, w_second, w_noise, w_volume):
    devices = lax.axis_size("inline") * lax.axis_size("xline")
    count, samples = traces.shape
    slots = devices * 8
    width = samples + TAIL
    vmem = pl.BlockSpec(memory_space=pltpu.VMEM)
    hbm = pl.BlockSpec(memory_space=pltpu.HBM)
    params = pltpu.CompilerParams(vmem_limit_bytes=24 << 20)
    rows = WIN * (-(-samples // WIN))
    outgoing = pl.pallas_call(
        denoise_kernel,
        out_shape=jax.ShapeDtypeStruct((slots, width), BF16),
        in_specs=[hbm] * 6,
        out_specs=hbm,
        scratch_shapes=[
            pltpu.VMEM((count, samples), BF16),
            pltpu.VMEM((1, count), jnp.int32),
            pltpu.VMEM((1, count), jnp.int32),
            pltpu.VMEM((3, 32), BF16),
            pltpu.VMEM((96, 32), BF16),
            pltpu.VMEM((1, 32), BF16),
            pltpu.VMEM((PAD + rows + 8, count), F32),
            pltpu.VMEM((rows, count), F32),
            pltpu.VMEM((4, 256, count), BF16),
            pltpu.VMEM((4, 256, count), BF16),
            pltpu.VMEM((768, 32), BF16),
            pltpu.VMEM((192, 256), BF16),
            pltpu.VMEM((64, count), F32),
            pltpu.VMEM((slots, width), BF16),
            pltpu.SemaphoreType.DMA((6,)),
            pltpu.SemaphoreType.DMA((samples // 256 + 1,)),
        ],
        compiler_params=pltpu.CompilerParams(vmem_limit_bytes=60 << 20),
        name="denoise",
    )(
        traces,
        owner.reshape(1, count),
        bin_ids.reshape(1, count),
        w_first.T,
        w_second.reshape(96, 32),
        w_noise.reshape(1, 32),
    )
    bins = BINS
    folds, w_taps = pl.pallas_call(
        prepare_kernel,
        out_shape=[jax.ShapeDtypeStruct((bins, TAIL), F32), jax.ShapeDtypeStruct((512, 12 * SIDE), BF16)],
        in_specs=[vmem] * 2,
        out_specs=[vmem] * 2,
        compiler_params=params,
        name="prepare",
    )(fold, w_volume)
    received = lax.all_to_all(
        outgoing.reshape(devices, 8, width), ("inline", "xline"), split_axis=0, concat_axis=0, tiled=True
    ).reshape(slots, width)
    edge = jax.ShapeDtypeStruct((STRIP, width), BF16)
    left, right = pl.pallas_call(
        sides_kernel,
        out_shape=[edge, edge],
        in_specs=[vmem] * 2,
        out_specs=[vmem] * 2,
        compiler_params=params,
        name="sides",
    )(received, folds)
    from_left, from_right = neighbours(left, right, "xline")
    main = pl.pallas_call(
        stack_kernel,
        out_shape=jax.ShapeDtypeStruct((width // 128, bins, 128), F32),
        in_specs=[vmem] * 2,
        out_specs=vmem,
        compiler_params=params,
        cost_estimate=pl.CostEstimate(flops=1 << 30, transcendentals=0, bytes_accessed=4 << 20),
        name="stack",
    )(received, folds)
    up, down = pl.pallas_call(
        edges_kernel,
        out_shape=[edge, edge],
        in_specs=[vmem] * 3,
        out_specs=[vmem] * 2,
        scratch_shapes=[pltpu.VMEM((STRIP, width), F32)] * 2,
        compiler_params=params,
        name="edges",
    )(main, from_left, from_right)
    above, below = neighbours(up, down, "inline")

    def scratch(slots):
        return [
            pltpu.VMEM((width // 128, bins, 128), F32),
            pltpu.VMEM((3, bins, samples), F32),
            pltpu.VMEM((slots, 2, 16, 16, samples), BF16),
            pltpu.SemaphoreType.DMA((slots, samples // 256)),
        ]

    features = jax.ShapeDtypeStruct((16, 16, 16, samples), BF16)
    inner = pl.pallas_call(
        inner_kernel,
        out_shape=features,
        in_specs=[vmem] * 4,
        out_specs=hbm,
        scratch_shapes=scratch(6),
        compiler_params=params,
        cost_estimate=pl.CostEstimate(flops=1 << 32, transcendentals=0, bytes_accessed=8 << 20),
        name="inner",
    )(main, from_left, from_right, w_taps)
    return pl.pallas_call(
        outer_kernel,
        out_shape=features,
        in_specs=[vmem] * 6 + [hbm],
        out_specs=hbm,
        scratch_shapes=scratch(2),
        input_output_aliases={6: 0},
        compiler_params=params,
        name="outer",
    )(main, from_left, from_right, above, below, w_taps, inner)


def solution(mesh):
    placed = (
        P(("inline", "xline"), None),
        P(("inline", "xline"), None),
        P(("inline", "xline")),
        P("inline", "xline"),
        P(),
        P(),
        P(),
        P(),
    )
    return jax.shard_map(
        body,
        mesh=mesh,
        in_specs=placed,
        out_specs=P("inline", None, "xline", None),
        check_vma=False,
    )
```

```python
import jax
import jax.numpy as jnp
from jax import lax
from jax.experimental import pallas as pl
from jax.experimental.pallas import tpu as pltpu
from jax.sharding import PartitionSpec as P

F32 = jnp.float32
BF16 = jnp.bfloat16
WIN = 24
PAD = 24
SIDE = 18
BINS = 328
EDGE = 2 * SIDE
STRIP = 40
TAIL = 128


def iota(shape, dim):
    return lax.broadcasted_iota(jnp.int32, shape, dim)


def picks(shape, row, col):
    return jnp.where(jnp.broadcast_to(row == col, shape), 1.0, 0.0).astype(BF16)


def column(vector, size):
    eye = iota((size, size), 0) == iota((size, size), 1)
    return jnp.sum(jnp.where(eye, vector, 0.0), axis=1, keepdims=True)


def denoise_kernel(*refs):
    ins, out_hbm, bufs = refs[:6], refs[6], refs[7:13]
    xt, dt, ha, hb, w1, w2, wn, wv, out_ref, in_sems, out_sems = refs[13:]
    x_ref, own_ref, bins_ref, wf_ref, ws_ref, wn_ref = bufs
    loads = [pltpu.make_async_copy(src, dst, in_sems.at[k]) for k, (src, dst) in enumerate(zip(ins, bufs))]
    for load in loads:
        load.start()
    traces, samples = x_ref.shape
    slots = out_ref.shape[0]
    rows = xt.shape[0]
    windows = -(-samples // WIN)
    hidden_bufs = (ha, hb)

    for load in loads:
        load.wait()

    own = own_ref[...]
    own_col = column(own.astype(F32), traces).astype(jnp.int32)
    earlier = (own_col == own) & (iota((traces, traces), 0) < iota((traces, traces), 1))
    rank = jnp.sum(jnp.where(earlier, 1.0, 0.0), axis=0, keepdims=True).astype(jnp.int32)
    placing = picks((slots, traces), iota((slots, traces), 0), own * 8 + rank)
    stores = []

    def place(start, width, rows):
        out_ref[:, start : start + width] = lax.dot_general(
            placing, rows, (((1,), (1,)), ((), ())), preferred_element_type=F32
        ).astype(BF16)
        store = pltpu.make_async_copy(
            out_ref.at[:, pl.ds(start, width)], out_hbm.at[:, pl.ds(start, width)], out_sems.at[len(stores)]
        )
        store.start()
        stores.append(store)

    wf = wf_ref[...].astype(F32)
    taps = [jnp.broadcast_to(column(wf[k : k + 1], 32), (32, 32)) for k in range(3)]
    for k in range(3):
        wv[k] = jnp.broadcast_to(taps[k][:, 0:1], (32, traces))
    lane = iota((32, 32), 1)
    for p in range(4):
        for u in range(6):
            block = jnp.zeros((32, 32), F32)
            for k in range(3):
                block = jnp.where(lane == 4 * u + p + k + 3, taps[k], block)
            w1[192 * p + 32 * u : 192 * p + 32 * (u + 1), :] = block.astype(BF16)
    wide = jnp.dot(
        ws_ref[...], picks((32, 256), iota((32, 256), 0), iota((32, 256), 1) % 32), preferred_element_type=F32
    ).astype(BF16)
    row = iota((192, 32), 0)
    channel = picks((192, 32), row % 64 // 8 * 4 + row % 4, iota((192, 32), 1))
    row = iota((192, 256), 0)
    apart = iota((192, 256), 1) // 32 - 2 * (row // 64) - row % 8 // 4
    total = jnp.zeros((192, 256), F32)
    for k in range(3):
        part = jnp.dot(channel, wide[32 * k : 32 * (k + 1)], preferred_element_type=F32)
        total = jnp.where(apart == k, part, total)
    w2[...] = total.astype(BF16)
    row = iota((64, 32), 0)
    of_row = jnp.where(row // 8 * 4 + row % 4 == iota((64, 32), 1), wn_ref[...].astype(F32), 0.0)
    wn[...] = jnp.broadcast_to(jnp.sum(of_row, axis=1, keepdims=True), wn.shape)

    xt[0:PAD, :] = jnp.zeros((PAD, traces), F32)
    xt[PAD + samples : rows, :] = jnp.zeros((rows - PAD - samples, traces), F32)
    for k in range(samples // 128):
        xt[PAD + 128 * k : PAD + 128 * (k + 1), :] = x_ref[:, 128 * k : 128 * (k + 1)].astype(F32).T

    def relu(value):
        return jnp.maximum(value.astype(BF16), jnp.zeros((), BF16))

    def hidden(j, h_ref, before):
        first = PAD + WIN * j
        xs = xt[first : first + 32, :].astype(BF16)
        for p in range(4):
            h_ref[p, 0:64, :] = before[p, 192:256, :]
        for u in range(6):
            at = first + 4 * u + 3
            value = wv[0] * xt[at : at + 1, :]
            for k in range(1, 3):
                value = value + wv[k] * xt[at + k : at + k + 1, :]
            h_ref[0, 64 + 32 * u : 96 + 32 * u, :] = relu(value)
        for p in range(1, 4):
            h_ref[p, 64:256, :] = relu(
                jnp.dot(w1[192 * p : 192 * (p + 1), :], xs, preferred_element_type=F32)
            )

    sub = iota((3, 8, traces), 1)
    even = (sub & 1) == 0
    low = (sub & 2) == 0

    def pair(a, b, shift, mask):
        return jnp.where(mask, a + pltpu.roll(a, 8 - shift, 1), b + pltpu.roll(b, shift, 1))

    def second(j, h_ref):
        parts = []
        for p in range(4):
            o = jnp.dot(w2[...], h_ref[p], preferred_element_type=F32)
            o = jnp.maximum(o, 0.0).reshape(3, 64, traces) * wn[...][None]
            parts.append(jnp.sum(o.reshape(3, 8, 8, traces), axis=1))
        noise = pair(pair(parts[0], parts[1], 1, even), pair(parts[2], parts[3], 1, even), 2, low)
        x = xt[PAD + WIN * j : PAD + WIN * (j + 1), :]
        dt[WIN * j : WIN * (j + 1), :] = x - noise.reshape(WIN, traces)

    xs = xt[PAD - WIN : PAD - WIN + 32, :].astype(BF16)
    for p in range(4):
        hb[p, 192:224, :] = jnp.zeros((32, traces), BF16)
        hb[p, 224:256, :] = relu(
            jnp.dot(w1[192 * p + 160 : 192 * (p + 1), :], xs, preferred_element_type=F32)
        )
    hidden(0, ha, hb)
    placed = 0
    which = iota((TAIL, traces), 0)
    row, col = bins_ref[...] // 18 + 1, bins_ref[...] % 18 + 1
    tail = jnp.where(which == 0, row, jnp.where(which == 1, col, 0)).astype(F32).astype(BF16)
    place(samples, TAIL, tail)
    for j in range(windows):
        this, other = hidden_bufs[j % 2], hidden_bufs[1 - j % 2]
        if j + 1 < windows:
            hidden(j + 1, other, this)
        else:
            inside = 32 * ((samples - WIN * j + 4) // 4)
            for p in range(4):
                this[p, inside:, :] = jnp.zeros((256 - inside, traces), BF16)
        second(j, this)
        ready = min(WIN * (j + 1), samples)
        while placed < samples:
            size = 128 if placed >= samples - 256 else 256
            if placed + size > ready:
                break
            place(placed, size, dt[placed : placed + size, :].astype(BF16))
            placed += size
    for store in stores:
        store.wait()


def prepare_kernel(fold_ref, wv_ref, fold_out, w_out):
    bins = fold_out.shape[0]
    row = iota((bins, 16), 0)
    of_x = jnp.dot(
        picks((bins, 16), row // SIDE - 1, iota((bins, 16), 1)),
        fold_ref[...].astype(F32).astype(BF16),
        preferred_element_type=F32,
    )
    own = jnp.sum(jnp.where(row % SIDE - 1 == iota((bins, 16), 1), of_x, 0.0), axis=1, keepdims=True)
    fold_out[...] = jnp.broadcast_to(own, fold_out.shape)
    rows, cols = w_out.shape
    by_row = jnp.dot(
        picks((rows, 16), iota((rows, 16), 0) // 16 % 16, iota((rows, 16), 1)),
        wv_ref[...],
        preferred_element_type=F32,
    ).astype(BF16)
    row, col = iota((rows, cols), 0), iota((rows, cols), 1)
    dx = col // SIDE % 4 - row // 256
    dy = col % SIDE - row % 16
    near = (dx >= 0) & (dx < 3)
    dt = iota((27, cols), 1) // (4 * SIDE)
    total = jnp.zeros((rows, cols), F32)
    for k in range(9):
        taps = picks((27, cols), 3 * k + dt, iota((27, cols), 0))
        part = jnp.dot(by_row, taps, preferred_element_type=F32)
        total = jnp.where(near & (dx == k // 3) & (dy == k % 3), part, total)
    w_out[...] = total.astype(BF16)


def bins_of(recv_ref):
    tail = recv_ref[:, recv_ref.shape[1] - TAIL :].astype(F32).T
    return ((tail[0:1] - 1.0) * SIDE + (tail[1:2] - 1.0)).astype(jnp.int32)


def sides_kernel(recv_ref, fold_ref, left_ref, right_ref):
    slots, width = recv_ref.shape
    row = iota((2 * STRIP, slots), 0)
    at = row % STRIP
    wanted_bin = at % SIDE * SIDE + at // SIDE + row // STRIP * 16
    wanted_bin = jnp.where(at < EDGE, wanted_bin, -1000)
    select = picks((2 * STRIP, slots), wanted_bin, bins_of(recv_ref))
    at = lax.axis_index("xline")
    sides = ((left_ref, 0, at > 0), (right_ref, 16, at < lax.axis_size("xline") - 1))
    for c in range(0, width - TAIL, 256):
        part = jnp.dot(select, recv_ref[:, c : c + 256], preferred_element_type=F32)
        for k, (ref, _, wanted) in enumerate(sides):
            ref[:, c : c + 256] = jnp.where(wanted, part[STRIP * k : STRIP * (k + 1)], 0.0).astype(BF16)
    pad = jnp.zeros((STRIP - EDGE, TAIL), F32)
    for ref, first, wanted in sides:
        cols = [fold_ref[pl.ds(first + k, SIDE, stride=SIDE), :] for k in range(2)]
        strip = jnp.concatenate([cols[0], cols[1], pad], axis=0)
        ref[:, width - TAIL :] = jnp.where(wanted, strip, 0.0).astype(BF16)


def stack_kernel(recv_ref, fold_ref, main_ref):
    slots = recv_ref.shape[0]
    blocks, bins, _ = main_ref.shape
    select = picks((bins, slots), iota((bins, slots), 0), bins_of(recv_ref))
    for c in range(0, blocks - 1, 2):
        both = jnp.dot(select, recv_ref[:, 128 * c : 128 * (c + 2)], preferred_element_type=F32)
        main_ref[c] = both[:, :128]
        main_ref[c + 1] = both[:, 128:]
    main_ref[blocks - 1] = fold_ref[...]


def edges_kernel(main_ref, left_ref, right_ref, up_ref, down_ref, up, down):
    blocks, bins, _ = main_ref.shape
    for c in range(blocks):
        lanes = slice(128 * c, 128 * (c + 1))
        up[:, lanes] = main_ref[c, 0:STRIP, :]
        down[:, lanes] = main_ref[c, bins - STRIP : bins, :]
    for ref, first in ((left_ref, 0), (right_ref, 16)):
        strip = ref[...].astype(F32)
        for k in range(2):
            for r in range(2):
                at = r * SIDE + first + k
                up[at : at + 1, :] += strip[SIDE * k + r : SIDE * k + r + 1, :]
                down[at : at + 1, :] += strip[SIDE * k + 16 + r : SIDE * k + 17 + r, :]
    at = lax.axis_index("inline")
    wanted = (iota(up.shape, 0) < EDGE) & (at > 0)
    up_ref[...] = jnp.where(wanted, up[...], 0.0).astype(BF16)
    down_ref[...] = jnp.where(at < lax.axis_size("inline") - 1, down[...], 0.0).astype(BF16)


def add_sides(acc, left_ref, right_ref, start, count):
    for c in range(acc.shape[0]):
        lanes = slice(128 * c, 128 * (c + 1))
        for ref, first in ((left_ref, 0), (right_ref, 16)):
            strip = ref[:, lanes].astype(F32)
            for k in range(2):
                rows = pl.ds(start * SIDE + first + k, count, stride=SIDE)
                acc[c, rows, :] += strip[SIDE * k + start : SIDE * k + start + count, :]


def make_taps(acc, vs, start, stop):
    blocks = acc.shape[0]
    samples = 128 * (blocks - 1)
    lane = iota((stop - start, samples), 1)
    fold = acc[blocks - 1, start:stop, :]
    inside = fold > 0.0
    fold = jnp.where(inside, fold, 1.0)
    v = jnp.concatenate([jnp.where(inside, acc[c, start:stop, :] / fold, 0.0) for c in range(blocks - 1)], axis=1)
    v = v.astype(BF16).astype(F32)
    vs[0, start:stop, :] = jnp.where(lane == 0, 0.0, pltpu.roll(v, 1, 1))
    vs[1, start:stop, :] = v
    vs[2, start:stop, :] = jnp.where(lane == samples - 1, 0.0, pltpu.roll(v, samples - 1, 1))


def convolve(m, vs, w_ref, block, out_hbm, sem, width):
    taps = jnp.concatenate([vs[dt, EDGE * m : EDGE * (m + 2), :] for dt in range(3)], axis=0).astype(BF16)
    stores = []
    for c in range(0, vs.shape[2], 256):
        part = jnp.dot(w_ref[...], taps[:, c : c + 256], preferred_element_type=F32)
        block[:, :, :, c : c + 256] = part.astype(BF16).reshape(2, 16, 16, 256)
        if (c + 256) % width == 0:
            lanes = pl.ds(c + 256 - width, width)
            store = pltpu.make_async_copy(
                block.at[:, :, :, lanes], out_hbm.at[pl.ds(2 * m, 2), :, :, lanes], sem.at[len(stores)]
            )
            store.start()
            stores.append(store)
    return stores


def inner_kernel(main_ref, left_ref, right_ref, w_ref, out_hbm, acc, vs, out, sems):
    acc[...] = main_ref[...]
    add_sides(acc, left_ref, right_ref, 2, 14)
    stores = []
    ends = [EDGE // 8 * 8] + [-(-EDGE * (m + 2) // 8) * 8 for m in range(1, 7)]
    make_taps(acc, vs, ends[0], ends[1])
    for k in range(6):
        if k < 5:
            make_taps(acc, vs, ends[k + 1], ends[k + 2])
        stores += convolve(k + 1, vs, w_ref, out.at[k], out_hbm, sems.at[k], 1024 if k < 5 else 512)
    for store in stores:
        store.wait()


def outer_kernel(main_ref, left_ref, right_ref, above_ref, below_ref, w_ref, _, out_hbm, acc, vs, out, sems):
    blocks, bins, _ = acc.shape
    top, bottom = 2 * EDGE, (bins - 2 * EDGE) // 8 * 8 - 8
    for c in range(blocks):
        lanes = slice(128 * c, 128 * (c + 1))
        acc[c, 0:top, :] = main_ref[c, 0:top, :]
        acc[c, bottom:bins, :] = main_ref[c, bottom:bins, :]
        acc[c, 0:STRIP, :] += above_ref[:, lanes].astype(F32)
        acc[c, bins - STRIP : bins, :] += below_ref[:, lanes].astype(F32)
    for start, stop, row in ((0, top, 0), (bottom, bins, 14)):
        add_sides(acc, left_ref, right_ref, row, 4)
        make_taps(acc, vs, start, stop)
    stores = convolve(0, vs, w_ref, out.at[0], out_hbm, sems.at[0], 512)
    stores += convolve(7, vs, w_ref, out.at[1], out_hbm, sems.at[1], 512)
    for store in stores:
        store.wait()


def neighbours(first, last, axis):
    size = lax.axis_size(axis)
    up = [(i, (i + 1) % size) for i in range(size)]
    down = [(j, i) for i, j in up]
    return lax.ppermute(last, axis, up), lax.ppermute(first, axis, down)


def body(traces, owner, bin_ids, fold, w_first, w_second, w_noise, w_volume):
    devices = lax.axis_size("inline") * lax.axis_size("xline")
    count, samples = traces.shape
    slots = devices * 8
    width = samples + TAIL
    vmem = pl.BlockSpec(memory_space=pltpu.VMEM)
    hbm = pl.BlockSpec(memory_space=pltpu.HBM)
    params = pltpu.CompilerParams(vmem_limit_bytes=24 << 20)
    rows = WIN * (-(-samples // WIN))
    outgoing = pl.pallas_call(
        denoise_kernel,
        out_shape=jax.ShapeDtypeStruct((slots, width), BF16),
        in_specs=[hbm] * 6,
        out_specs=hbm,
        scratch_shapes=[
            pltpu.VMEM((count, samples), BF16),
            pltpu.VMEM((1, count), jnp.int32),
            pltpu.VMEM((1, count), jnp.int32),
            pltpu.VMEM((3, 32), BF16),
            pltpu.VMEM((96, 32), BF16),
            pltpu.VMEM((1, 32), BF16),
            pltpu.VMEM((PAD + rows + 8, count), F32),
            pltpu.VMEM((rows, count), F32),
            pltpu.VMEM((4, 256, count), BF16),
            pltpu.VMEM((4, 256, count), BF16),
            pltpu.VMEM((768, 32), BF16),
            pltpu.VMEM((192, 256), BF16),
            pltpu.VMEM((64, count), F32),
            pltpu.VMEM((3, 32, count), F32),
            pltpu.VMEM((slots, width), BF16),
            pltpu.SemaphoreType.DMA((6,)),
            pltpu.SemaphoreType.DMA((samples // 256 + 2,)),
        ],
        compiler_params=pltpu.CompilerParams(vmem_limit_bytes=60 << 20),
        name="denoise",
    )(
        traces,
        owner.reshape(1, count),
        bin_ids.reshape(1, count),
        w_first.T,
        w_second.reshape(96, 32),
        w_noise.reshape(1, 32),
    )
    bins = BINS
    folds, w_taps = pl.pallas_call(
        prepare_kernel,
        out_shape=[jax.ShapeDtypeStruct((bins, TAIL), F32), jax.ShapeDtypeStruct((512, 12 * SIDE), BF16)],
        in_specs=[vmem] * 2,
        out_specs=[vmem] * 2,
        compiler_params=params,
        name="prepare",
    )(fold, w_volume)
    received = lax.all_to_all(
        outgoing.reshape(devices, 8, width), ("inline", "xline"), split_axis=0, concat_axis=0, tiled=True
    ).reshape(slots, width)
    edge = jax.ShapeDtypeStruct((STRIP, width), BF16)
    left, right = pl.pallas_call(
        sides_kernel,
        out_shape=[edge, edge],
        in_specs=[vmem] * 2,
        out_specs=[vmem] * 2,
        compiler_params=params,
        name="sides",
    )(received, folds)
    from_left, from_right = neighbours(left, right, "xline")
    main = pl.pallas_call(
        stack_kernel,
        out_shape=jax.ShapeDtypeStruct((width // 128, bins, 128), F32),
        in_specs=[vmem] * 2,
        out_specs=vmem,
        compiler_params=params,
        cost_estimate=pl.CostEstimate(flops=1 << 30, transcendentals=0, bytes_accessed=4 << 20),
        name="stack",
    )(received, folds)
    up, down = pl.pallas_call(
        edges_kernel,
        out_shape=[edge, edge],
        in_specs=[vmem] * 3,
        out_specs=[vmem] * 2,
        scratch_shapes=[pltpu.VMEM((STRIP, width), F32)] * 2,
        compiler_params=params,
        name="edges",
    )(main, from_left, from_right)
    above, below = neighbours(up, down, "inline")

    def scratch(slots):
        return [
            pltpu.VMEM((width // 128, bins, 128), F32),
            pltpu.VMEM((3, bins, samples), F32),
            pltpu.VMEM((slots, 2, 16, 16, samples), BF16),
            pltpu.SemaphoreType.DMA((slots, samples // 256)),
        ]

    features = jax.ShapeDtypeStruct((16, 16, 16, samples), BF16)
    inner = pl.pallas_call(
        inner_kernel,
        out_shape=features,
        in_specs=[vmem] * 4,
        out_specs=hbm,
        scratch_shapes=scratch(6),
        compiler_params=params,
        cost_estimate=pl.CostEstimate(flops=1 << 32, transcendentals=0, bytes_accessed=8 << 20),
        name="inner",
    )(main, from_left, from_right, w_taps)
    return pl.pallas_call(
        outer_kernel,
        out_shape=features,
        in_specs=[vmem] * 6 + [hbm],
        out_specs=hbm,
        scratch_shapes=scratch(2),
        input_output_aliases={6: 0},
        compiler_params=params,
        name="outer",
    )(main, from_left, from_right, above, below, w_taps, inner)


def solution(mesh):
    placed = (
        P(("inline", "xline"), None),
        P(("inline", "xline"), None),
        P(("inline", "xline")),
        P("inline", "xline"),
        P(),
        P(),
        P(),
        P(),
    )
    return jax.shard_map(
        body,
        mesh=mesh,
        in_specs=placed,
        out_specs=P("inline", None, "xline", None),
        check_vma=False,
    )
```

```python
import jax
import jax.numpy as jnp
from jax import lax
from jax.experimental import pallas as pl
from jax.experimental.pallas import tpu as pltpu
from jax.sharding import PartitionSpec as P

F32 = jnp.float32
BF16 = jnp.bfloat16
WIN = 24
PAD = 24
SIDE = 18
BINS = 328
EDGE = 2 * SIDE
STRIP = 40
TAIL = 128


def iota(shape, dim):
    return lax.broadcasted_iota(jnp.int32, shape, dim)


def picks(shape, row, col):
    return jnp.where(jnp.broadcast_to(row == col, shape), 1.0, 0.0).astype(BF16)


def column(vector, size):
    eye = iota((size, size), 0) == iota((size, size), 1)
    return jnp.sum(jnp.where(eye, vector, 0.0), axis=1, keepdims=True)


def denoise_kernel(*refs):
    ins, out_hbm, bufs = refs[:6], refs[6], refs[7:13]
    xt, dt, ha, hb, w1, w2, wn, wv, out_ref, in_sems, out_sems = refs[13:]
    x_ref, own_ref, bins_ref, wf_ref, ws_ref, wn_ref = bufs
    loads = [pltpu.make_async_copy(src, dst, in_sems.at[k]) for k, (src, dst) in enumerate(zip(ins, bufs))]
    for load in loads:
        load.start()
    traces, samples = x_ref.shape
    slots = out_ref.shape[0]
    rows = xt.shape[0]
    windows = -(-samples // WIN)
    hidden_bufs = (ha, hb)

    for load in loads:
        load.wait()

    own = own_ref[...]
    own_col = column(own.astype(F32), traces).astype(jnp.int32)
    earlier = (own_col == own) & (iota((traces, traces), 0) < iota((traces, traces), 1))
    rank = jnp.sum(jnp.where(earlier, 1.0, 0.0), axis=0, keepdims=True).astype(jnp.int32)
    placing = picks((slots, traces), iota((slots, traces), 0), own * 8 + rank)
    stores = []

    def place(start, width, rows):
        out_ref[:, start : start + width] = lax.dot_general(
            placing, rows, (((1,), (1,)), ((), ())), preferred_element_type=F32
        ).astype(BF16)
        store = pltpu.make_async_copy(
            out_ref.at[:, pl.ds(start, width)], out_hbm.at[:, pl.ds(start, width)], out_sems.at[len(stores)]
        )
        store.start()
        stores.append(store)

    wf = wf_ref[...].astype(F32)
    taps = [jnp.broadcast_to(column(wf[k : k + 1], 32), (32, 32)) for k in range(3)]
    for k in range(3):
        wv[k] = jnp.broadcast_to(taps[k][:, 0:1], (32, traces))
    lane = iota((32, 32), 1)
    for p in range(4):
        for u in range(6):
            block = jnp.zeros((32, 32), F32)
            for k in range(3):
                block = jnp.where(lane == 4 * u + p + k + 3, taps[k], block)
            w1[192 * p + 32 * u : 192 * p + 32 * (u + 1), :] = block.astype(BF16)
    wide = jnp.dot(
        ws_ref[...], picks((32, 256), iota((32, 256), 0), iota((32, 256), 1) % 32), preferred_element_type=F32
    ).astype(BF16)
    row = iota((192, 32), 0)
    channel = picks((192, 32), row % 64 // 8 * 4 + row % 4, iota((192, 32), 1))
    row = iota((192, 256), 0)
    apart = iota((192, 256), 1) // 32 - 2 * (row // 64) - row % 8 // 4
    total = jnp.zeros((192, 256), F32)
    for k in range(3):
        part = jnp.dot(channel, wide[32 * k : 32 * (k + 1)], preferred_element_type=F32)
        total = jnp.where(apart == k, part, total)
    w2[...] = total.astype(BF16)
    row = iota((64, 32), 0)
    of_row = jnp.where(row // 8 * 4 + row % 4 == iota((64, 32), 1), wn_ref[...].astype(F32), 0.0)
    wn[...] = jnp.broadcast_to(jnp.sum(of_row, axis=1, keepdims=True), wn.shape)

    xt[0:PAD, :] = jnp.zeros((PAD, traces), F32)
    xt[PAD + samples : rows, :] = jnp.zeros((rows - PAD - samples, traces), F32)
    for k in range(samples // 128):
        xt[PAD + 128 * k : PAD + 128 * (k + 1), :] = x_ref[:, 128 * k : 128 * (k + 1)].astype(F32).T

    def relu(value):
        return jnp.maximum(value.astype(BF16), jnp.zeros((), BF16))

    def hidden(j, h_ref, before, steps=6):
        first = PAD + WIN * j
        xs = xt[first : first + 32, :].astype(BF16)
        for p in range(4):
            h_ref[p, 0:64, :] = before[p, 192:256, :]
        for u in range(steps):
            at = first + 4 * u + 3
            value = wv[0] * xt[at : at + 1, :]
            for k in range(1, 3):
                value = value + wv[k] * xt[at + k : at + k + 1, :]
            h_ref[0, 64 + 32 * u : 96 + 32 * u, :] = relu(value)
        for p in range(1, 4):
            h_ref[p, 64 : 64 + 32 * steps, :] = relu(
                jnp.dot(w1[192 * p : 192 * p + 32 * steps, :], xs, preferred_element_type=F32)
            )

    def pair(a, b, shift, mask):
        return jnp.where(mask, a + pltpu.roll(a, 8 - shift, 1), b + pltpu.roll(b, shift, 1))

    def second(j, h_ref, tiles=3):
        sub = iota((tiles, 8, traces), 1)
        even, low = (sub & 1) == 0, (sub & 2) == 0
        parts = []
        for p in range(4):
            o = jnp.dot(w2[0 : 64 * tiles, :], h_ref[p], preferred_element_type=F32)
            o = jnp.maximum(o, 0.0).reshape(tiles, 64, traces) * wn[...][None]
            parts.append(jnp.sum(o.reshape(tiles, 8, 8, traces), axis=1))
        noise = pair(pair(parts[0], parts[1], 1, even), pair(parts[2], parts[3], 1, even), 2, low)
        size = 8 * tiles
        x = xt[PAD + WIN * j : PAD + WIN * j + size, :]
        dt[WIN * j : WIN * j + size, :] = x - noise.reshape(size, traces)

    xs = xt[PAD - WIN : PAD - WIN + 32, :].astype(BF16)
    for p in range(4):
        hb[p, 192:224, :] = jnp.zeros((32, traces), BF16)
        hb[p, 224:256, :] = relu(
            jnp.dot(w1[192 * p + 160 : 192 * (p + 1), :], xs, preferred_element_type=F32)
        )
    hidden(0, ha, hb)
    placed = 0
    tiles = -(-(samples - WIN * (windows - 1)) // 8)
    steps = (samples - WIN * (windows - 1) + 4) // 4
    which = iota((TAIL, traces), 0)
    row, col = bins_ref[...] // 18 + 1, bins_ref[...] % 18 + 1
    tail = jnp.where(which == 0, row, jnp.where(which == 1, col, 0)).astype(F32).astype(BF16)
    place(samples, TAIL, tail)
    for j in range(windows):
        this, other = hidden_bufs[j % 2], hidden_bufs[1 - j % 2]
        if j + 1 < windows:
            hidden(j + 1, other, this, 6 if j + 2 < windows else steps - 2)
        else:
            inside = 32 * steps
            for p in range(4):
                this[p, inside:, :] = jnp.zeros((256 - inside, traces), BF16)
        second(j, this, 3 if j + 1 < windows else tiles)
        ready = min(WIN * (j + 1), samples)
        while placed < samples:
            size = 128 if placed >= samples - 256 else 256
            if placed + size > ready:
                break
            place(placed, size, dt[placed : placed + size, :].astype(BF16))
            placed += size
    for store in stores:
        store.wait()


def prepare_kernel(fold_ref, wv_ref, fold_out, w_out):
    bins = fold_out.shape[0]
    row = iota((bins, 16), 0)
    of_x = jnp.dot(
        picks((bins, 16), row // SIDE - 1, iota((bins, 16), 1)),
        fold_ref[...].astype(F32).astype(BF16),
        preferred_element_type=F32,
    )
    own = jnp.sum(jnp.where(row % SIDE - 1 == iota((bins, 16), 1), of_x, 0.0), axis=1, keepdims=True)
    fold_out[...] = jnp.broadcast_to(own, fold_out.shape)
    rows, cols = w_out.shape
    by_row = jnp.dot(
        picks((rows, 16), iota((rows, 16), 0) // 16 % 16, iota((rows, 16), 1)),
        wv_ref[...],
        preferred_element_type=F32,
    ).astype(BF16)
    row, col = iota((rows, cols), 0), iota((rows, cols), 1)
    dx = col // SIDE % 4 - row // 256
    dy = col % SIDE - row % 16
    near = (dx >= 0) & (dx < 3)
    dt = iota((27, cols), 1) // (4 * SIDE)
    total = jnp.zeros((rows, cols), F32)
    for k in range(9):
        taps = picks((27, cols), 3 * k + dt, iota((27, cols), 0))
        part = jnp.dot(by_row, taps, preferred_element_type=F32)
        total = jnp.where(near & (dx == k // 3) & (dy == k % 3), part, total)
    w_out[...] = total.astype(BF16)


def bins_of(recv_ref):
    tail = recv_ref[:, recv_ref.shape[1] - TAIL :].astype(F32).T
    return ((tail[0:1] - 1.0) * SIDE + (tail[1:2] - 1.0)).astype(jnp.int32)


def sides_kernel(recv_ref, fold_ref, left_ref, right_ref):
    slots, width = recv_ref.shape
    row = iota((2 * STRIP, slots), 0)
    at = row % STRIP
    wanted_bin = at % SIDE * SIDE + at // SIDE + row // STRIP * 16
    wanted_bin = jnp.where(at < EDGE, wanted_bin, -1000)
    select = picks((2 * STRIP, slots), wanted_bin, bins_of(recv_ref))
    at = lax.axis_index("xline")
    sides = ((left_ref, 0, at > 0), (right_ref, 16, at < lax.axis_size("xline") - 1))
    for c in range(0, width - TAIL, 256):
        part = jnp.dot(select, recv_ref[:, c : c + 256], preferred_element_type=F32)
        for k, (ref, _, wanted) in enumerate(sides):
            ref[:, c : c + 256] = jnp.where(wanted, part[STRIP * k : STRIP * (k + 1)], 0.0).astype(BF16)
    pad = jnp.zeros((STRIP - EDGE, TAIL), F32)
    for ref, first, wanted in sides:
        cols = [fold_ref[pl.ds(first + k, SIDE, stride=SIDE), :] for k in range(2)]
        strip = jnp.concatenate([cols[0], cols[1], pad], axis=0)
        ref[:, width - TAIL :] = jnp.where(wanted, strip, 0.0).astype(BF16)


def stack_kernel(recv_ref, fold_ref, main_ref):
    slots = recv_ref.shape[0]
    blocks, bins, _ = main_ref.shape
    select = picks((bins, slots), iota((bins, slots), 0), bins_of(recv_ref))
    for c in range(0, blocks - 1, 2):
        both = jnp.dot(select, recv_ref[:, 128 * c : 128 * (c + 2)], preferred_element_type=F32)
        main_ref[c] = both[:, :128]
        main_ref[c + 1] = both[:, 128:]
    main_ref[blocks - 1] = fold_ref[...]


def edges_kernel(main_ref, left_ref, right_ref, up_ref, down_ref, up, down):
    blocks, bins, _ = main_ref.shape
    for c in range(blocks):
        lanes = slice(128 * c, 128 * (c + 1))
        up[:, lanes] = main_ref[c, 0:STRIP, :]
        down[:, lanes] = main_ref[c, bins - STRIP : bins, :]
    for ref, first in ((left_ref, 0), (right_ref, 16)):
        strip = ref[...].astype(F32)
        for k in range(2):
            for r in range(2):
                at = r * SIDE + first + k
                up[at : at + 1, :] += strip[SIDE * k + r : SIDE * k + r + 1, :]
                down[at : at + 1, :] += strip[SIDE * k + 16 + r : SIDE * k + 17 + r, :]
    at = lax.axis_index("inline")
    wanted = (iota(up.shape, 0) < EDGE) & (at > 0)
    up_ref[...] = jnp.where(wanted, up[...], 0.0).astype(BF16)
    down_ref[...] = jnp.where(at < lax.axis_size("inline") - 1, down[...], 0.0).astype(BF16)


def add_sides(acc, left_ref, right_ref, start, count):
    for c in range(acc.shape[0]):
        lanes = slice(128 * c, 128 * (c + 1))
        for ref, first in ((left_ref, 0), (right_ref, 16)):
            strip = ref[:, lanes].astype(F32)
            for k in range(2):
                rows = pl.ds(start * SIDE + first + k, count, stride=SIDE)
                acc[c, rows, :] += strip[SIDE * k + start : SIDE * k + start + count, :]


def make_taps(acc, vs, start, stop):
    blocks = acc.shape[0]
    samples = 128 * (blocks - 1)
    lane = iota((stop - start, samples), 1)
    fold = acc[blocks - 1, start:stop, :]
    inside = fold > 0.0
    fold = jnp.where(inside, fold, 1.0)
    v = jnp.concatenate([jnp.where(inside, acc[c, start:stop, :] / fold, 0.0) for c in range(blocks - 1)], axis=1)
    v = v.astype(BF16).astype(F32)
    vs[0, start:stop, :] = jnp.where(lane == 0, 0.0, pltpu.roll(v, 1, 1))
    vs[1, start:stop, :] = v
    vs[2, start:stop, :] = jnp.where(lane == samples - 1, 0.0, pltpu.roll(v, samples - 1, 1))


def convolve(m, vs, w_ref, block, out_hbm, sem, width):
    taps = jnp.concatenate([vs[dt, EDGE * m : EDGE * (m + 2), :] for dt in range(3)], axis=0).astype(BF16)
    stores = []
    for c in range(0, vs.shape[2], 256):
        part = jnp.dot(w_ref[...], taps[:, c : c + 256], preferred_element_type=F32)
        block[:, :, :, c : c + 256] = part.astype(BF16).reshape(2, 16, 16, 256)
        if (c + 256) % width == 0:
            lanes = pl.ds(c + 256 - width, width)
            store = pltpu.make_async_copy(
                block.at[:, :, :, lanes], out_hbm.at[pl.ds(2 * m, 2), :, :, lanes], sem.at[len(stores)]
            )
            store.start()
            stores.append(store)
    return stores


def inner_kernel(main_ref, left_ref, right_ref, w_ref, out_hbm, acc, vs, out, sems):
    first, last = EDGE // 8 * 8, -(-16 * SIDE // 8) * 8
    cut = -(-EDGE * 3 // 8) * 8

    def assemble(start, stop, row, count):
        for c in range(acc.shape[0]):
            acc[c, start:stop, :] = main_ref[c, start:stop, :]
        add_sides(acc, left_ref, right_ref, row, count)

    assemble(first, cut, 2, 4)
    make_taps(acc, vs, first, cut)
    stores = convolve(1, vs, w_ref, out.at[0], out_hbm, sems.at[0], 512)
    assemble(cut - 8, last, 5, 11)
    ends = [cut - 8] + [-(-EDGE * (m + 2) // 8) * 8 for m in range(2, 7)]
    make_taps(acc, vs, ends[0], ends[1])
    for k in range(1, 6):
        if k < 5:
            make_taps(acc, vs, ends[k], ends[k + 1])
        stores += convolve(k + 1, vs, w_ref, out.at[k], out_hbm, sems.at[k], 1024 if k < 5 else 512)
    for store in stores:
        store.wait()


def outer_kernel(main_ref, left_ref, right_ref, above_ref, below_ref, w_ref, _, out_hbm, acc, vs, out, sems):
    blocks, bins, _ = acc.shape
    top, bottom = 2 * EDGE, (bins - 2 * EDGE) // 8 * 8 - 8
    for c in range(blocks):
        lanes = slice(128 * c, 128 * (c + 1))
        acc[c, 0:top, :] = main_ref[c, 0:top, :]
        acc[c, bottom:bins, :] = main_ref[c, bottom:bins, :]
        acc[c, 0:STRIP, :] += above_ref[:, lanes].astype(F32)
        acc[c, bins - STRIP : bins, :] += below_ref[:, lanes].astype(F32)
    for start, stop, row in ((0, top, 0), (bottom, bins, 14)):
        add_sides(acc, left_ref, right_ref, row, 4)
        make_taps(acc, vs, start, stop)
    stores = convolve(0, vs, w_ref, out.at[0], out_hbm, sems.at[0], 512)
    stores += convolve(7, vs, w_ref, out.at[1], out_hbm, sems.at[1], 512)
    for store in stores:
        store.wait()


def neighbours(first, last, axis):
    size = lax.axis_size(axis)
    up = [(i, (i + 1) % size) for i in range(size)]
    down = [(j, i) for i, j in up]
    return lax.ppermute(last, axis, up), lax.ppermute(first, axis, down)


def body(traces, owner, bin_ids, fold, w_first, w_second, w_noise, w_volume):
    devices = lax.axis_size("inline") * lax.axis_size("xline")
    count, samples = traces.shape
    slots = devices * 8
    width = samples + TAIL
    vmem = pl.BlockSpec(memory_space=pltpu.VMEM)
    hbm = pl.BlockSpec(memory_space=pltpu.HBM)
    params = pltpu.CompilerParams(vmem_limit_bytes=24 << 20)
    rows = WIN * (-(-samples // WIN))
    outgoing = pl.pallas_call(
        denoise_kernel,
        out_shape=jax.ShapeDtypeStruct((slots, width), BF16),
        in_specs=[hbm] * 6,
        out_specs=hbm,
        scratch_shapes=[
            pltpu.VMEM((count, samples), BF16),
            pltpu.VMEM((1, count), jnp.int32),
            pltpu.VMEM((1, count), jnp.int32),
            pltpu.VMEM((3, 32), BF16),
            pltpu.VMEM((96, 32), BF16),
            pltpu.VMEM((1, 32), BF16),
            pltpu.VMEM((PAD + rows + 8, count), F32),
            pltpu.VMEM((rows, count), F32),
            pltpu.VMEM((4, 256, count), BF16),
            pltpu.VMEM((4, 256, count), BF16),
            pltpu.VMEM((768, 32), BF16),
            pltpu.VMEM((192, 256), BF16),
            pltpu.VMEM((64, count), F32),
            pltpu.VMEM((3, 32, count), F32),
            pltpu.VMEM((slots, width), BF16),
            pltpu.SemaphoreType.DMA((6,)),
            pltpu.SemaphoreType.DMA((samples // 256 + 2,)),
        ],
        compiler_params=pltpu.CompilerParams(vmem_limit_bytes=60 << 20),
        name="denoise",
    )(
        traces,
        owner.reshape(1, count),
        bin_ids.reshape(1, count),
        w_first.T,
        w_second.reshape(96, 32),
        w_noise.reshape(1, 32),
    )
    bins = BINS
    folds, w_taps = pl.pallas_call(
        prepare_kernel,
        out_shape=[jax.ShapeDtypeStruct((bins, TAIL), F32), jax.ShapeDtypeStruct((512, 12 * SIDE), BF16)],
        in_specs=[vmem] * 2,
        out_specs=[vmem] * 2,
        compiler_params=params,
        name="prepare",
    )(fold, w_volume)
    received = lax.all_to_all(
        outgoing.reshape(devices, 8, width), ("inline", "xline"), split_axis=0, concat_axis=0, tiled=True
    ).reshape(slots, width)
    edge = jax.ShapeDtypeStruct((STRIP, width), BF16)
    left, right = pl.pallas_call(
        sides_kernel,
        out_shape=[edge, edge],
        in_specs=[vmem] * 2,
        out_specs=[vmem] * 2,
        compiler_params=params,
        name="sides",
    )(received, folds)
    from_left, from_right = neighbours(left, right, "xline")
    main = pl.pallas_call(
        stack_kernel,
        out_shape=jax.ShapeDtypeStruct((width // 128, bins, 128), F32),
        in_specs=[vmem] * 2,
        out_specs=vmem,
        compiler_params=params,
        cost_estimate=pl.CostEstimate(flops=1 << 30, transcendentals=0, bytes_accessed=4 << 20),
        name="stack",
    )(received, folds)
    up, down = pl.pallas_call(
        edges_kernel,
        out_shape=[edge, edge],
        in_specs=[vmem] * 3,
        out_specs=[vmem] * 2,
        scratch_shapes=[pltpu.VMEM((STRIP, width), F32)] * 2,
        compiler_params=params,
        name="edges",
    )(main, from_left, from_right)
    above, below = neighbours(up, down, "inline")

    def scratch(slots):
        return [
            pltpu.VMEM((width // 128, bins, 128), F32),
            pltpu.VMEM((3, bins, samples), F32),
            pltpu.VMEM((slots, 2, 16, 16, samples), BF16),
            pltpu.SemaphoreType.DMA((slots, samples // 256)),
        ]

    features = jax.ShapeDtypeStruct((16, 16, 16, samples), BF16)
    inner = pl.pallas_call(
        inner_kernel,
        out_shape=features,
        in_specs=[vmem] * 4,
        out_specs=hbm,
        scratch_shapes=scratch(6),
        compiler_params=params,
        cost_estimate=pl.CostEstimate(flops=1 << 32, transcendentals=0, bytes_accessed=8 << 20),
        name="inner",
    )(main, from_left, from_right, w_taps)
    return pl.pallas_call(
        outer_kernel,
        out_shape=features,
        in_specs=[vmem] * 6 + [hbm],
        out_specs=hbm,
        scratch_shapes=scratch(2),
        input_output_aliases={6: 0},
        compiler_params=params,
        name="outer",
    )(main, from_left, from_right, above, below, w_taps, inner)


def solution(mesh):
    placed = (
        P(("inline", "xline"), None),
        P(("inline", "xline"), None),
        P(("inline", "xline")),
        P("inline", "xline"),
        P(),
        P(),
        P(),
        P(),
    )
    return jax.shard_map(
        body,
        mesh=mesh,
        in_specs=placed,
        out_specs=P("inline", None, "xline", None),
        check_vma=False,
    )
```
